128 devices in a mesh: row: 8 (over z, x_lo), col: 16 (over y, x_hi, core).
Axes of the slice: x: 4 (x_hi: 2, x_lo: 2; x = x_hi * 2 + x_lo), y: 4, z: 4, core: 2. Of those that a mesh axis runs over, the one named last changes fastest.
Arguments:
- tensor_blocks: bfloat16 [8, 384, 6, 128, 128], P('row', 'col'), may hold values from -6 to 6
- block_list: int32 [8, 384, 2], P('row', 'col'), may hold values from 0 to 15, as said below
- occ_green: bfloat16 [2048, 2048], P(('row', 'col')), may hold values from -0.125 to 0.125
- virt_green: bfloat16 [2048, 2048], P(None, ('row', 'col')), may hold values from -0.125 to 0.125
Outputs:
- polarizability: float32 [8, 6, 6], P('row')
The draws below stay inside these ranges and needn't reach their ends.
Inputs may be any that keep to these rules, and one draw needn't show every extreme that they name: `block_list`: within the 24 blocks of one device the (m, l) pairs are distinct, every atom block occurs as l once or twice and as m once or twice, so at most 2 blocks of one device share an l, and some l is shared by exactly 2.
All inputs are finite; a program needn't handle non-finite values.
Results may differ from the reference program's by a relative error of at most 0.006.
Values may be sent and summed in bfloat16 or wider, within the bound.
No kernel may reach another device: no remote copies, remote signals or barrier semaphores. Data moves between devices by JAX's collectives and lax.ppermute only.
A program may use at most 128 MiB of HBM per device.

```python
import jax
import jax.numpy as jnp
from jax import lax

BS = 128
PA = 6
TB_DEV = 24
NAO = 2048
N_ROW = 8
N_COL = 16


def draw_block_list(key, part):

    def one_device(device_number):
        device_key = jax.random.fold_in(key, device_number)
        second_order = jax.random.permutation(jax.random.fold_in(device_key, 1), N_COL)
        first_order = jax.random.permutation(jax.random.fold_in(device_key, 2), N_COL)
        places = jnp.arange(TB_DEV)
        first_index = first_order[(places + places // N_COL) % N_COL]
        second_index = second_order[places % N_COL]
        return jnp.stack([first_index, second_index], axis=1)
    lists = jax.vmap(one_device)(jnp.arange(N_ROW * N_COL))
    return lists.reshape(N_ROW, N_COL * TB_DEV, 2).astype(jnp.int32)


def shard_levels(stream_key, dims, shards, least, top_value):
    def one(dim, shards_of):
        heights = jax.random.uniform(jax.random.fold_in(jax.random.fold_in(stream_key, 6), dim), (shards_of,), jnp.float32, least / len(shards), top_value / len(shards))
        return jnp.repeat(jnp.exp(heights), dims[dim] // shards_of).reshape((-1,) + (1,) * (len(dims) - dim - 1))

    loudness = one(*shards[0])
    for cut in shards[1:]:
        loudness = loudness * one(*cut)
    return loudness


def centred(stream_key, dims, width, limit, cuts=(), dtype=jnp.bfloat16):
    drawn = jax.random.normal(stream_key, dims, jnp.float32) * width
    if len(cuts) > 0:
        drawn = shard_levels(stream_key, dims, cuts, -0.22, 0.18) * drawn
    return jnp.clip(drawn, min=-limit, max=limit).astype(dtype)


def setup_inputs(seed: int = 0) -> dict:
    arg_keys = jax.random.split(jax.random.key(seed), 5)
    return {
        "tensor_blocks": centred(arg_keys[0], (N_ROW, N_COL * TB_DEV, PA, BS, BS), 1.0, 6.0, ((0, 8), (1, 16))),
        "block_list": draw_block_list(jax.random.fold_in(arg_keys[4], 71), 0),
        "occ_green": centred(arg_keys[2], (NAO, NAO), NAO ** -0.5, 0.125, ((0, 128),)),
        "virt_green": centred(arg_keys[3], (NAO, NAO), NAO ** -0.5, 0.125, ((1, 128),)),
    }


def reference(tensor_blocks, block_list, occ_green, virt_green):
    occ_wide = occ_green.astype(jnp.float32)
    virt_wide = virt_green.astype(jnp.float32)

    def group_work(group_args):
        blocks, pairs = group_args
        index = (pairs[:, 0] * N_COL + pairs[:, 1]).astype(jnp.int32)
        summed = jax.ops.segment_sum(blocks.astype(jnp.float32), index, num_segments=N_COL * N_COL)
        summed = summed.reshape(N_COL, N_COL, PA, BS, BS)
        dense_tensor = jnp.transpose(summed, (2, 0, 3, 1, 4)).reshape(PA, NAO, NAO).astype(jnp.bfloat16)
        dense_wide = dense_tensor.astype(jnp.float32)
        occ_half = jnp.einsum('nm,pml->pnl', occ_wide, dense_wide).astype(jnp.bfloat16)
        both_sides = jnp.einsum('pnl,ls->pns', occ_half.astype(jnp.float32), virt_wide).astype(jnp.bfloat16)
        return jnp.einsum('pns,qsn->pq', both_sides.astype(jnp.float32), dense_wide) / float(NAO)

    return lax.map(group_work, (tensor_blocks, block_list))
```

```python
import functools

import jax
import jax.numpy as jnp
from jax import lax
from jax.experimental import pallas as pl
from jax.experimental.pallas import tpu as pltpu
from jax.sharding import Mesh
from jax.sharding import PartitionSpec as P

CAP = 2
CHUNKS = 2
AXES = ("z", "xl", "y", "xh", "core")
SIZES = (4, 2, 4, 2, 2)
COL = ("y", "xh", "core")
ROW = ("z", "xl")
PLANE = ("xl", "y", "xh")


def moved(axis, to):
    where = AXES.index(axis)
    stride = 1
    for size in SIZES[where + 1 :]:
        stride *= size
    total = 1
    for size in SIZES:
        total *= size
    pairs = []
    for device in range(total):
        k = device // stride % SIZES[where]
        pairs.append((device, device + (to(k) - k) * stride))
    return pairs


def permute(x, axis, to):
    return lax.ppermute(x, AXES, moved(axis, to))


def up(x):
    return permute(x, "z", lambda k: (k + 1) % 4)


def down(x):
    return permute(x, "z", lambda k: (k - 1) % 4)


def other_core(x):
    return permute(x, "core", lambda k: 1 - k)


def pick_kernel(chunks, pairs_ref, blocks_ref, *refs):
    out_refs = refs[:chunks]
    first_ref, count, sems = refs[chunks:]
    held = blocks_ref.shape[0]
    depth = blocks_ref.shape[1] // chunks
    owners = first_ref.shape[0]
    for d in range(owners):
        count[d] = 0
        for k in range(CAP):
            first_ref[d, k] = -1
    copies = []
    for t in range(held):
        l = pairs_ref[t, 1]
        k = count[l]
        count[l] = k + 1
        first_ref[l, k] = pairs_ref[t, 0]
        for c in range(chunks):
            copy = pltpu.make_async_copy(
                blocks_ref.at[t, pl.ds(c * depth, depth)], out_refs[c].at[l, k], sems.at[t, c]
            )
            copy.start()
            copies.append(copy)
    for copy in copies:
        copy.wait()


def pick(pairs, blocks, owners):
    held, aux, width, _ = blocks.shape
    depth = aux // CHUNKS
    out = jax.ShapeDtypeStruct((owners, CAP, depth, width, width), blocks.dtype)
    return pl.pallas_call(
        functools.partial(pick_kernel, CHUNKS),
        out_shape=[out] * CHUNKS + [jax.ShapeDtypeStruct((owners, CAP), jnp.int32)],
        in_specs=[
            pl.BlockSpec(memory_space=pltpu.SMEM),
            pl.BlockSpec(memory_space=pl.ANY),
        ],
        out_specs=[pl.BlockSpec(memory_space=pl.ANY)] * CHUNKS
        + [pl.BlockSpec(memory_space=pltpu.SMEM)],
        scratch_shapes=[
            pltpu.SMEM((owners,), jnp.int32),
            pltpu.SemaphoreType.DMA((held, CHUNKS)),
        ],
        cost_estimate=pl.CostEstimate(flops=0, bytes_accessed=4 * blocks.size, transcendentals=0),
        name="pick",
    )(pairs, blocks)


def place_kernel(first_ref, blocks_ref, out_ref, total):
    slots, width = blocks_ref.shape[0], blocks_ref.shape[-1]
    total[...] = jnp.zeros_like(total)

    def body(s, carry):
        m = first_ref[s]

        @pl.when(m >= 0)
        def _():
            rows = pl.ds(pl.multiple_of(m * width, width), width)
            total[rows, :] += blocks_ref[s, 0].astype(jnp.float32)

        return carry

    lax.fori_loop(0, slots, body, 0)
    out_ref[...] = total[...].astype(out_ref.dtype)


def place(first, blocks, rows):
    slots, depth, width, _ = blocks.shape
    return pl.pallas_call(
        place_kernel,
        out_shape=jax.ShapeDtypeStruct((rows, depth * width), blocks.dtype),
        grid_spec=pltpu.PrefetchScalarGridSpec(
            num_scalar_prefetch=1,
            grid=(depth,),
            in_specs=[pl.BlockSpec((slots, 1, width, width), lambda p, first: (0, p, 0, 0))],
            out_specs=pl.BlockSpec((rows, width), lambda p, first: (0, p)),
            scratch_shapes=[pltpu.VMEM((rows, width), jnp.float32)],
        ),
        compiler_params=pltpu.CompilerParams(vmem_limit_bytes=32 * 1024 * 1024),
        cost_estimate=pl.CostEstimate(
            flops=blocks.size, bytes_accessed=4 * blocks.size, transcendentals=0
        ),
        name="place",
    )(first, blocks)


def lay_kernel(*refs):
    pieces, out_ref, sems = refs[:-2], refs[-2], refs[-1]
    z, core = lax.axis_index("z"), lax.axis_index("core")
    half = out_ref.shape[1] // 2
    full = out_ref.shape[1]
    spots = [
        (0, 0, full),
        (3, 0, full),
        (1, 0, full),
        (2, 0, half),
        (2, half, half),
    ]
    copies = []
    for side in range(2):
        for i, (dz, start, size) in enumerate(spots):
            n = side * len(spots) + i
            copy = pltpu.make_async_copy(
                pieces[n],
                out_ref.at[(z + dz) % 4, pl.ds(start, size), (core + side) % 2],
                sems.at[n],
            )
            copy.start()
            copies.append(copy)
    for copy in copies:
        copy.wait()


def lay(pieces):
    plane, rows, columns = pieces[0].shape
    return pl.pallas_call(
        lay_kernel,
        out_shape=jax.ShapeDtypeStruct((4, plane, 2, rows, columns), pieces[0].dtype),
        in_specs=[pl.BlockSpec(memory_space=pl.ANY)] * len(pieces),
        out_specs=pl.BlockSpec(memory_space=pl.ANY),
        scratch_shapes=[pltpu.SemaphoreType.DMA((len(pieces),))],
        cost_estimate=pl.CostEstimate(
            flops=0, bytes_accessed=32 * pieces[0].size, transcendentals=0
        ),
        name="lay",
    )(*pieces).reshape(8 * plane * rows, columns)


def plane_gather(shard):
    count = 16
    copies = jnp.broadcast_to(shard[None], (count, *shard.shape))
    return lax.all_to_all(copies, PLANE, split_axis=0, concat_axis=0, tiled=True)


def z_gather(mine):
    half = mine.shape[0] // 2
    from_below, from_above = up(mine), down(mine)
    far_low, far_high = up(from_below[:half]), down(from_above[half:])
    pieces = [mine, from_below, from_above, far_low, far_high]
    return lay(pieces + [other_core(p) for p in pieces])


def pair_kernel(x_ref, y_ref, out_ref):
    width = x_ref.shape[1]
    aux_x, aux_y = x_ref.shape[2] // width, y_ref.shape[0] // width

    @pl.when(pl.program_id(0) == 0)
    def _():
        out_ref[...] = jnp.zeros_like(out_ref)

    for p in range(aux_x):
        x = x_ref[0, :, p * width : (p + 1) * width].astype(jnp.float32)
        for q in range(aux_y):
            y = y_ref[q * width : (q + 1) * width, :].astype(jnp.float32)
            out_ref[p * aux_y + q] += (x * y).reshape(width // 8, 8, width).sum(axis=0)


def pair_sums(x, y):
    blocks, width, _ = x.shape
    aux_x, aux_y = x.shape[2] // width, y.shape[0] // width
    sums = pl.pallas_call(
        pair_kernel,
        out_shape=jax.ShapeDtypeStruct((aux_x * aux_y, 8, width), jnp.float32),
        grid=(blocks,),
        in_specs=[
            pl.BlockSpec((1, width, aux_x * width), lambda k: (k, 0, 0)),
            pl.BlockSpec((aux_y * width, width), lambda k: (0, k)),
        ],
        out_specs=pl.BlockSpec((aux_x * aux_y, 8, width), lambda k: (0, 0, 0)),
        cost_estimate=pl.CostEstimate(
            flops=2 * x.size * aux_y, bytes_accessed=2 * (x.size + y.size), transcendentals=0
        ),
        name="pair",
    )(x, y)
    return sums.sum(axis=(1, 2)).reshape(aux_x, aux_y)


def col_sum(x):
    x = x + other_core(x)
    x = x + permute(x, "xh", lambda k: 1 - k)
    x = x + permute(x, "y", lambda k: k ^ 1)
    return x + permute(x, "y", lambda k: k ^ 2)


def shards(tensor_blocks, block_list, occ_green, virt_green):
    col_count = lax.axis_size(COL)
    blocks = tensor_blocks[0]
    width = blocks.shape[-1]
    basis_total = occ_green.shape[1]

    both = jnp.concatenate([occ_green, virt_green.T], axis=0)
    both_plane = plane_gather(both)
    shard_rows = occ_green.shape[0]
    occ = z_gather(both_plane[:, :shard_rows])
    virt_t = z_gather(both_plane[:, shard_rows:])

    *picked, send_first = pick(block_list[0], blocks, col_count)
    recv = [
        lax.all_to_all(part, COL, split_axis=0, concat_axis=0, tiled=True) for part in picked
    ]
    recv_first = lax.all_to_all(
        send_first[:, None], COL, split_axis=0, concat_axis=0, tiled=True
    ).reshape(-1)

    dense, turned = [], []
    for part in recv:
        part = part.reshape(-1, *part.shape[2:])
        dense.append(place(recv_first, part, basis_total))
        half = jnp.dot(occ, dense[-1], preferred_element_type=jnp.float32).astype(jnp.bfloat16)
        half = half.reshape(col_count, width, -1)
        turned.append(lax.all_to_all(half, COL, split_axis=0, concat_axis=0, tiled=True))

    virt_half = jnp.concatenate(
        [
            lax.dot_general(
                d, virt_t, (((0,), (0,)), ((), ())), preferred_element_type=jnp.float32
            ).astype(jnp.bfloat16)
            for d in dense
        ],
        axis=0,
    )
    sums = jnp.concatenate([pair_sums(x, virt_half) for x in turned], axis=0)
    return (col_sum(sums) / float(basis_total))[None]


def solution(mesh):
    fine = Mesh(mesh.devices.reshape(SIZES), AXES)
    in_specs = (
        P(ROW, COL, None, None, None),
        P(ROW, COL, None),
        P(ROW + COL, None),
        P(None, ROW + COL),
    )
    return jax.shard_map(
        shards, mesh=fine, in_specs=in_specs, out_specs=P(ROW, None, None), check_vma=False
    )
```

```python
import functools

import jax
import jax.numpy as jnp
from jax import lax
from jax.experimental import pallas as pl
from jax.experimental.pallas import tpu as pltpu
from jax.sharding import Mesh
from jax.sharding import PartitionSpec as P

CAP = 2
CHUNKS = 2
AXES = ("z", "xl", "y", "xh", "core")
SIZES = (4, 2, 4, 2, 2)
COL = ("y", "xh", "core")
ROW = ("z", "xl")


def moved(axis, to):
    where = AXES.index(axis)
    stride = 1
    for size in SIZES[where + 1 :]:
        stride *= size
    total = 1
    for size in SIZES:
        total *= size
    pairs = []
    for device in range(total):
        k = device // stride % SIZES[where]
        pairs.append((device, device + (to(k) - k) * stride))
    return pairs


def permute(x, axis, to):
    return lax.ppermute(x, AXES, moved(axis, to))


def up(x):
    return permute(x, "z", lambda k: (k + 1) % 4)


def down(x):
    return permute(x, "z", lambda k: (k - 1) % 4)


def other_core(x):
    return permute(x, "core", lambda k: 1 - k)


def pick_kernel(chunks, pairs_ref, blocks_ref, *refs):
    out_refs = refs[:chunks]
    stage, count, in_sems, out_sems = refs[chunks:]
    held = blocks_ref.shape[0]
    depth = blocks_ref.shape[1] // chunks
    loads = [
        pltpu.make_async_copy(blocks_ref.at[t], stage.at[t], in_sems.at[t]) for t in range(held)
    ]
    for load in loads:
        load.start()
    for d in range(count.shape[0]):
        count[d] = 0
    stores = []
    for t in range(held):
        l = pairs_ref[t, 1]
        k = count[l]
        count[l] = k + 1
        loads[t].wait()
        for c in range(chunks):
            store = pltpu.make_async_copy(
                stage.at[t, pl.ds(c * depth, depth)], out_refs[c].at[l, k], out_sems.at[t, c]
            )
            store.start()
            stores.append(store)
    for store in stores:
        store.wait()


def pick(pairs, blocks, owners):
    held, aux, width, _ = blocks.shape
    depth = aux // CHUNKS
    out = jax.ShapeDtypeStruct((owners, CAP, depth, width, width), blocks.dtype)
    return pl.pallas_call(
        functools.partial(pick_kernel, CHUNKS),
        out_shape=[out] * CHUNKS,
        in_specs=[
            pl.BlockSpec(memory_space=pltpu.SMEM),
            pl.BlockSpec(memory_space=pl.ANY),
        ],
        out_specs=[pl.BlockSpec(memory_space=pl.ANY)] * CHUNKS,
        scratch_shapes=[
            pltpu.VMEM(blocks.shape, blocks.dtype),
            pltpu.SMEM((owners,), jnp.int32),
            pltpu.SemaphoreType.DMA((held,)),
            pltpu.SemaphoreType.DMA((held, CHUNKS)),
        ],
        compiler_params=pltpu.CompilerParams(vmem_limit_bytes=8 * 1024 * 1024),
        cost_estimate=pl.CostEstimate(flops=0, bytes_accessed=4 * blocks.size, transcendentals=0),
        name="pick",
    )(pairs, blocks)


def firsts_for_me(all_pairs):
    hit = all_pairs[:, :, 1] == lax.axis_index(COL)
    places = jnp.arange(all_pairs.shape[1])
    before = places[None, :] < places[:, None]
    rank = jnp.sum(hit[:, None, :] & before[None], axis=2)
    chosen = hit[:, :, None] & (rank[:, :, None] == jnp.arange(CAP))
    return jnp.sum(jnp.where(chosen, all_pairs[:, :, :1] + 1, 0), axis=1).reshape(-1) - 1


def place_kernel(first_ref, blocks_ref, out_ref, total):
    slots, width = blocks_ref.shape[0], blocks_ref.shape[-1]
    total[...] = jnp.zeros_like(total)

    def body(s, carry):
        m = first_ref[s]

        @pl.when(m >= 0)
        def _():
            rows = pl.ds(pl.multiple_of(m * width, width), width)
            total[rows, :] += blocks_ref[s, 0].astype(jnp.float32)

        return carry

    lax.fori_loop(0, slots, body, 0)
    out_ref[...] = total[...].astype(out_ref.dtype)


def place(first, blocks, rows):
    slots, depth, width, _ = blocks.shape
    return pl.pallas_call(
        place_kernel,
        out_shape=jax.ShapeDtypeStruct((rows, depth * width), blocks.dtype),
        grid_spec=pltpu.PrefetchScalarGridSpec(
            num_scalar_prefetch=1,
            grid=(depth,),
            in_specs=[pl.BlockSpec((slots, 1, width, width), lambda p, first: (0, p, 0, 0))],
            out_specs=pl.BlockSpec((rows, width), lambda p, first: (0, p)),
            scratch_shapes=[pltpu.VMEM((rows, width), jnp.float32)],
        ),
        compiler_params=pltpu.CompilerParams(vmem_limit_bytes=8 * 1024 * 1024),
        cost_estimate=pl.CostEstimate(
            flops=blocks.size, bytes_accessed=4 * blocks.size, transcendentals=0
        ),
        name="place",
    )(first, blocks)


def lay_kernel(spots, *refs):
    pieces, out_ref, sem = refs[:-2], refs[-2], refs[-1]
    z, y, core = lax.axis_index("z"), lax.axis_index("y"), lax.axis_index("core")
    x = 2 * lax.axis_index("xh") + lax.axis_index("xl")
    for piece, (side, dz, chips) in zip(pieces, spots, strict=True):
        for i, (dx, dy) in enumerate(chips):
            to_x = (x + dx) % 4
            pltpu.make_async_copy(
                piece.at[i],
                out_ref.at[(z + dz) % 4, to_x % 2, (y + dy) % 4, to_x // 2, (core + side) % 2],
                sem,
            ).start()
    pltpu.make_async_copy(out_ref, out_ref, sem).wait()


def lay(spots, pieces):
    _, rows, columns = pieces[0].shape
    out = pl.pallas_call(
        functools.partial(lay_kernel, spots),
        out_shape=jax.ShapeDtypeStruct((*SIZES, rows, columns), pieces[0].dtype),
        in_specs=[pl.BlockSpec(memory_space=pl.ANY)] * len(pieces),
        out_specs=pl.BlockSpec(memory_space=pltpu.VMEM),
        scratch_shapes=[pltpu.SemaphoreType.DMA],
        compiler_params=pltpu.CompilerParams(vmem_limit_bytes=12 * 1024 * 1024),
        cost_estimate=pl.CostEstimate(
            flops=0, bytes_accessed=512 * rows * columns, transcendentals=0
        ),
        name="lay",
    )(*pieces)
    return out.reshape(-1, columns)


def ring(x, move):
    return jnp.concatenate([x, move(x, 1), move(x, -1), move(x, 2)], axis=0)


FROM = (0, -1, 1, 2)


def y_move(x, by):
    return permute(x, "y", lambda k: (k + by) % 4)


def x_move(x, by):
    pairs = []
    for device in range(128):
        xl, xh = device // 16 % 2, device // 2 % 2
        to = (2 * xh + xl + by) % 4
        pairs.append((device, device + (to % 2 - xl) * 16 + (to // 2 - xh) * 2))
    return lax.ppermute(x, AXES, pairs)


def gather(shard, chips, first, second):
    mine = ring(ring(shard[None], first), second)
    half = mine.shape[0] // 2
    from_below, from_above = up(mine), down(mine)
    far_low, far_high = up(from_below[:half]), down(from_above[half:])
    pieces = [mine, from_below, from_above, far_low, far_high]
    spots = [(0, chips), (-1, chips), (1, chips), (2, chips[:half]), (2, chips[half:])]
    spots = [(side, dz, those) for side in range(2) for dz, those in spots]
    return lay(spots, pieces + [other_core(p) for p in pieces])


def pair_kernel(x_ref, y_ref, out_ref):
    width = x_ref.shape[1]
    aux_x, aux_y = x_ref.shape[2] // width, y_ref.shape[0] // width
    step = 16

    @pl.when(pl.program_id(0) == 0)
    def _():
        out_ref[...] = jnp.zeros_like(out_ref)

    def body(r, totals):
        rows = pl.multiple_of(r * step, step)
        ys = [y_ref[pl.ds(rows + q * width, step), :].astype(jnp.float32) for q in range(aux_y)]
        news = []
        for p in range(aux_x):
            x = x_ref[0, pl.ds(rows, step), p * width : (p + 1) * width].astype(jnp.float32)
            for q in range(aux_y):
                xy = x * ys[q]
                news.append(totals[p * aux_y + q] + (xy[:8] + xy[8:]))
        return tuple(news)

    zero = jnp.zeros((8, width), jnp.float32)
    totals = lax.fori_loop(0, width // step, body, (zero,) * (aux_x * aux_y), unroll=2)
    for i, total in enumerate(totals):
        out_ref[i] += total


def pair_sums(x, y):
    blocks, width, _ = x.shape
    aux_x, aux_y = x.shape[2] // width, y.shape[0] // width
    sums = pl.pallas_call(
        pair_kernel,
        out_shape=jax.ShapeDtypeStruct((aux_x * aux_y, 8, width), jnp.float32),
        grid=(blocks,),
        in_specs=[
            pl.BlockSpec((1, width, aux_x * width), lambda k: (k, 0, 0)),
            pl.BlockSpec((aux_y * width, width), lambda k: (0, k)),
        ],
        out_specs=pl.BlockSpec((aux_x * aux_y, 8, width), lambda k: (0, 0, 0)),
        cost_estimate=pl.CostEstimate(
            flops=2 * x.size * aux_y, bytes_accessed=2 * (x.size + y.size), transcendentals=0
        ),
        name="pair",
    )(x, y)
    return sums.sum(axis=(1, 2)).reshape(aux_x, aux_y)


def col_sum(x):
    x = x + other_core(x)
    x = x + permute(x, "xh", lambda k: 1 - k)
    x = x + permute(x, "y", lambda k: k ^ 1)
    return x + permute(x, "y", lambda k: k ^ 2)


def shards(tensor_blocks, block_list, occ_green, virt_green):
    col_count = lax.axis_size(COL)
    blocks = tensor_blocks[0]
    width = blocks.shape[-1]
    basis_total = occ_green.shape[1]

    all_pairs = lax.all_gather(block_list[0], COL, axis=0)
    recv_first = firsts_for_me(all_pairs)

    by_xy = tuple((dx, dy) for dx in FROM for dy in FROM)
    by_yx = tuple((dx, dy) for dy in FROM for dx in FROM)
    occ = gather(occ_green, by_xy, y_move, x_move)
    virt_t = gather(virt_green.T, by_yx, x_move, y_move)

    picked = pick(block_list[0], blocks, col_count)
    recv = [
        lax.all_to_all(part, COL, split_axis=0, concat_axis=0, tiled=True) for part in picked
    ]

    dense, turned = [], []
    for part in recv:
        part = part.reshape(-1, *part.shape[2:])
        dense.append(place(recv_first, part, basis_total))
        half = jnp.dot(occ, dense[-1], preferred_element_type=jnp.float32).astype(jnp.bfloat16)
        half = half.reshape(col_count, width, -1)
        turned.append(lax.all_to_all(half, COL, split_axis=0, concat_axis=0, tiled=True))

    virt_half = jnp.concatenate(
        [
            lax.dot_general(
                d, virt_t, (((0,), (0,)), ((), ())), preferred_element_type=jnp.float32
            ).astype(jnp.bfloat16)
            for d in dense
        ],
        axis=0,
    )
    sums = jnp.concatenate([pair_sums(x, virt_half) for x in turned], axis=0)
    return (col_sum(sums) / float(basis_total))[None]


def solution(mesh):
    fine = Mesh(mesh.devices.reshape(SIZES), AXES)
    in_specs = (
        P(ROW, COL, None, None, None),
        P(ROW, COL, None),
        P(ROW + COL, None),
        P(None, ROW + COL),
    )
    return jax.shard_map(
        shards, mesh=fine, in_specs=in_specs, out_specs=P(ROW, None, None), check_vma=False
    )
```

```python
import functools

import jax
import jax.numpy as jnp
from jax import lax
from jax.experimental import pallas as pl
from jax.experimental.pallas import tpu as pltpu
from jax.sharding import Mesh
from jax.sharding import PartitionSpec as P

CAP = 2
CHUNKS = 2
NOTE = 16
AXES = ("z", "xl", "y", "xh", "core")
SIZES = (4, 2, 4, 2, 2)
COL = ("y", "xh", "core")
ROW = ("z", "xl")


def moved(axis, to):
    where = AXES.index(axis)
    stride = 1
    for size in SIZES[where + 1 :]:
        stride *= size
    total = 1
    for size in SIZES:
        total *= size
    pairs = []
    for device in range(total):
        k = device // stride % SIZES[where]
        pairs.append((device, device + (to(k) - k) * stride))
    return pairs


def permute(x, axis, to):
    return lax.ppermute(x, AXES, moved(axis, to))


def up(x):
    return permute(x, "z", lambda k: (k + 1) % 4)


def down(x):
    return permute(x, "z", lambda k: (k - 1) % 4)


def other_core(x):
    return permute(x, "core", lambda k: 1 - k)


def pick_kernel(pairs_ref, blocks_ref, out_ref, count, first):
    held, rows, width = blocks_ref.shape
    owners = count.shape[0]
    for d in range(owners):
        count[d] = 0
        for k in range(CAP):
            first[d, k] = 0

    def body(t, carry):
        l = pairs_ref[t, 1]
        k = count[l]
        count[l] = k + 1
        first[l, k] = pairs_ref[t, 0] + 1
        out_ref[l, pl.ds(pl.multiple_of(k * rows, rows), rows), :] = blocks_ref[t]
        return carry

    lax.fori_loop(0, held, body, 0)
    which = lax.broadcasted_iota(jnp.int32, (NOTE, width), 0)
    for d in range(owners):
        note = jnp.zeros((NOTE, width), jnp.float32)
        for k in range(CAP):
            note = jnp.where(which == k, first[d, k].astype(jnp.float32), note)
        out_ref[d, CAP * rows :, :] = note.astype(out_ref.dtype)


def pick(pairs, blocks, owners):
    held, aux, width, _ = blocks.shape
    rows = aux * width
    return pl.pallas_call(
        pick_kernel,
        out_shape=jax.ShapeDtypeStruct((owners, CAP * rows + NOTE, width), blocks.dtype),
        in_specs=[
            pl.BlockSpec(memory_space=pltpu.SMEM),
            pl.BlockSpec(memory_space=pltpu.VMEM),
        ],
        out_specs=pl.BlockSpec(memory_space=pltpu.VMEM),
        scratch_shapes=[
            pltpu.SMEM((owners,), jnp.int32),
            pltpu.SMEM((owners, CAP), jnp.int32),
        ],
        compiler_params=pltpu.CompilerParams(vmem_limit_bytes=16 * 1024 * 1024),
        cost_estimate=pl.CostEstimate(flops=0, bytes_accessed=4 * blocks.size, transcendentals=0),
        name="pick",
    )(pairs, blocks.reshape(held, rows, width))


def place_kernel(first_ref, *refs):
    slot_refs, out_ref, total = refs[:CAP], refs[CAP], refs[CAP + 1]
    width = total.shape[1]
    total[...] = jnp.zeros_like(total)

    def body(s, carry):
        for k, slots in enumerate(slot_refs):
            m = first_ref[s * CAP + k]

            @pl.when(m >= 0)
            def _():
                rows = pl.ds(pl.multiple_of(m * width, width), width)
                total[rows, :] += slots[s].astype(jnp.float32)

        return carry

    lax.fori_loop(0, slot_refs[0].shape[0], body, 0)
    out_ref[...] = total[...].astype(out_ref.dtype)


def place(first, recv, start, depth, aux, rows):
    senders, _, width = recv.shape

    def slot(k):
        return pl.BlockSpec((senders, width, width), lambda p, first: (0, k * aux + start + p, 0))

    size = senders * CAP * depth * width * width
    return pl.pallas_call(
        place_kernel,
        out_shape=jax.ShapeDtypeStruct((rows, depth * width), recv.dtype),
        grid_spec=pltpu.PrefetchScalarGridSpec(
            num_scalar_prefetch=1,
            grid=(depth,),
            in_specs=[slot(k) for k in range(CAP)],
            out_specs=pl.BlockSpec((rows, width), lambda p, first: (0, p)),
            scratch_shapes=[pltpu.VMEM((rows, width), jnp.float32)],
        ),
        compiler_params=pltpu.CompilerParams(vmem_limit_bytes=8 * 1024 * 1024),
        cost_estimate=pl.CostEstimate(flops=size, bytes_accessed=4 * size, transcendentals=0),
        name="place",
    )(first, *[recv] * CAP)


def lay_kernel(spots, *refs):
    pieces, out_ref, sem = refs[:-2], refs[-2], refs[-1]
    z, y, core = lax.axis_index("z"), lax.axis_index("y"), lax.axis_index("core")
    x = 2 * lax.axis_index("xh") + lax.axis_index("xl")
    for piece, (side, dz, chips) in zip(pieces, spots, strict=True):
        for i, (dx, dy) in enumerate(chips):
            to_x = (x + dx) % 4
            pltpu.make_async_copy(
                piece.at[i],
                out_ref.at[(z + dz) % 4, to_x % 2, (y + dy) % 4, to_x // 2, (core + side) % 2],
                sem,
            ).start()
    pltpu.make_async_copy(out_ref, out_ref, sem).wait()


def lay(spots, pieces):
    _, rows, columns = pieces[0].shape
    out = pl.pallas_call(
        functools.partial(lay_kernel, spots),
        out_shape=jax.ShapeDtypeStruct((*SIZES, rows, columns), pieces[0].dtype),
        in_specs=[pl.BlockSpec(memory_space=pl.ANY)] * len(pieces),
        out_specs=pl.BlockSpec(memory_space=pltpu.VMEM),
        scratch_shapes=[pltpu.SemaphoreType.DMA],
        compiler_params=pltpu.CompilerParams(vmem_limit_bytes=12 * 1024 * 1024),
        cost_estimate=pl.CostEstimate(
            flops=0, bytes_accessed=512 * rows * columns, transcendentals=0
        ),
        name="lay",
    )(*pieces)
    return out.reshape(-1, columns)


def ring(x, move):
    return jnp.concatenate([x, move(x, 1), move(x, -1), move(x, 2)], axis=0)


FROM = (0, -1, 1, 2)


def y_move(x, by):
    return permute(x, "y", lambda k: (k + by) % 4)


def x_move(x, by):
    pairs = []
    for device in range(128):
        xl, xh = device // 16 % 2, device // 2 % 2
        to = (2 * xh + xl + by) % 4
        pairs.append((device, device + (to % 2 - xl) * 16 + (to // 2 - xh) * 2))
    return lax.ppermute(x, AXES, pairs)


def plane_gather(shard, first, second):
    return ring(ring(shard[None], first), second)


def z_near(mine):
    return up(mine), down(mine)


def z_far(mine, near):
    half = mine.shape[0] // 2
    return up(near[0][:half]), down(near[1][half:])


def assemble(mine, near, far, chips):
    half = mine.shape[0] // 2
    pieces = [mine, *near, *far]
    spots = [(0, chips), (-1, chips), (1, chips), (2, chips[:half]), (2, chips[half:])]
    spots = [(side, dz, those) for side in range(2) for dz, those in spots]
    return lay(spots, pieces + [other_core(p) for p in pieces])


def pair_kernel(x_ref, *refs):
    y_refs, out_ref = refs[:-1], refs[-1]
    blocks, width, _ = x_ref.shape
    aux_x = x_ref.shape[2] // width
    same = lax.broadcasted_iota(jnp.int32, (width, width), 0) == lax.broadcasted_iota(
        jnp.int32, (width, width), 1
    )
    x = jnp.concatenate(
        [
            jnp.concatenate(
                [x_ref[k, :, p * width : (p + 1) * width] for k in range(blocks)], axis=1
            )
            for p in range(aux_x)
        ],
        axis=0,
    )
    done = 0
    for y_ref in y_refs:
        products = lax.dot_general(
            x, y_ref[...], (((1,), (1,)), ((), ())), preferred_element_type=jnp.float32
        )
        aux_y = y_ref.shape[0] // width
        for q in range(aux_y):
            for p in range(aux_x):
                tile = products[p * width : (p + 1) * width, q * width : (q + 1) * width]
                tile = jnp.where(same, tile, 0.0).reshape(width // 8, 8, width)
                out_ref[(done + q) * aux_x + p] = tile.sum(axis=0)
        done += aux_y


def pair_sums(x, ys):
    _, width, _ = x.shape
    aux_x, aux_y = x.shape[2] // width, sum(y.shape[0] for y in ys) // width
    sums = pl.pallas_call(
        pair_kernel,
        out_shape=jax.ShapeDtypeStruct((aux_y * aux_x, 8, width), jnp.float32),
        in_specs=[pl.BlockSpec(memory_space=pltpu.VMEM)] * (1 + len(ys)),
        out_specs=pl.BlockSpec(memory_space=pltpu.VMEM),
        compiler_params=pltpu.CompilerParams(vmem_limit_bytes=16 * 1024 * 1024),
        cost_estimate=pl.CostEstimate(
            flops=2 * x.size * aux_y, bytes_accessed=6 * x.size, transcendentals=0
        ),
        name="pair",
    )(x, *ys)
    return sums.sum(axis=(1, 2)).reshape(aux_y, aux_x).T


def col_sum(x):
    x = x + other_core(x)
    x = x + permute(x, "xh", lambda k: 1 - k)
    x = x + permute(x, "y", lambda k: k ^ 1)
    return x + permute(x, "y", lambda k: k ^ 2)


def shards(tensor_blocks, block_list, occ_green, virt_green):
    col_count = lax.axis_size(COL)
    blocks = tensor_blocks[0]
    aux, width = blocks.shape[1], blocks.shape[-1]
    depth = aux // CHUNKS
    basis_total = occ_green.shape[1]

    by_xy = tuple((dx, dy) for dx in FROM for dy in FROM)
    by_yx = tuple((dx, dy) for dy in FROM for dx in FROM)
    occ_plane = plane_gather(occ_green, y_move, x_move)
    occ_near = z_near(occ_plane)
    occ_near, virt_shard = lax.optimization_barrier((occ_near, virt_green.T))
    occ_far = z_far(occ_plane, occ_near)
    virt_plane = plane_gather(virt_shard, x_move, y_move)
    occ_far, virt_plane = lax.optimization_barrier((occ_far, virt_plane))
    virt_near = z_near(virt_plane)
    virt_far = z_far(virt_plane, virt_near)
    occ = assemble(occ_plane, occ_near, occ_far, by_xy)
    virt_t = assemble(virt_plane, virt_near, virt_far, by_yx)

    picked = pick(block_list[0], blocks, col_count)
    recv = lax.all_to_all(picked, COL, split_axis=0, concat_axis=0, tiled=True)
    notes = CAP * aux * width
    recv_first = recv[:, notes : notes + CAP, 0].astype(jnp.int32).reshape(-1) - 1

    dense, turned = [], []
    for c in range(CHUNKS):
        dense.append(place(recv_first, recv, c * depth, depth, aux, basis_total))
        half = jnp.dot(occ, dense[-1], preferred_element_type=jnp.float32).astype(jnp.bfloat16)
        half = half.reshape(col_count, width, -1)
        turned.append(lax.all_to_all(half, COL, split_axis=0, concat_axis=0, tiled=True))

    virt_half = [
        lax.dot_general(
            d, virt_t, (((0,), (0,)), ((), ())), preferred_element_type=jnp.float32
        ).astype(jnp.bfloat16)
        for d in dense
    ]
    sums = jnp.concatenate([pair_sums(x, virt_half) for x in turned], axis=0)
    return (col_sum(sums) / float(basis_total))[None]


def solution(mesh):
    fine = Mesh(mesh.devices.reshape(SIZES), AXES)
    in_specs = (
        P(ROW, COL, None, None, None),
        P(ROW, COL, None),
        P(ROW + COL, None),
        P(None, ROW + COL),
    )
    return jax.shard_map(
        shards, mesh=fine, in_specs=in_specs, out_specs=P(ROW, None, None), check_vma=False
    )
```

```python
import functools

import jax
import jax.numpy as jnp
from jax import lax
from jax.experimental import pallas as pl
from jax.experimental.pallas import tpu as pltpu
from jax.sharding import Mesh
from jax.sharding import PartitionSpec as P

CAP = 2
CHUNKS = (2, 4)
NOTE = 16
AXES = ("z", "xl", "y", "xh", "core")
SIZES = (4, 2, 4, 2, 2)
COL = ("y", "xh", "core")
ROW = ("z", "xl")


def moved(axis, to):
    where = AXES.index(axis)
    stride = 1
    for size in SIZES[where + 1 :]:
        stride *= size
    total = 1
    for size in SIZES:
        total *= size
    pairs = []
    for device in range(total):
        k = device // stride % SIZES[where]
        pairs.append((device, device + (to(k) - k) * stride))
    return pairs


def permute(x, axis, to):
    return lax.ppermute(x, AXES, moved(axis, to))


def up(x):
    return permute(x, "z", lambda k: (k + 1) % 4)


def down(x):
    return permute(x, "z", lambda k: (k - 1) % 4)


def other_core(x):
    return permute(x, "core", lambda k: 1 - k)


def pick_kernel(pairs_ref, blocks_ref, out_ref, count, first):
    held, rows, width = blocks_ref.shape
    owners = count.shape[0]
    for d in range(owners):
        count[d] = 0
        for k in range(CAP):
            first[d, k] = 0

    def body(t, carry):
        l = pairs_ref[t, 1]
        k = count[l]
        count[l] = k + 1
        first[l, k] = pairs_ref[t, 0] + 1
        out_ref[l, pl.ds(pl.multiple_of(k * rows, rows), rows), :] = blocks_ref[t]
        return carry

    lax.fori_loop(0, held, body, 0)
    which = lax.broadcasted_iota(jnp.int32, (NOTE, width), 0)
    for d in range(owners):
        note = jnp.zeros((NOTE, width), jnp.float32)
        for k in range(CAP):
            note = jnp.where(which == k, first[d, k].astype(jnp.float32), note)
        out_ref[d, CAP * rows :, :] = note.astype(out_ref.dtype)


def pick(pairs, blocks, owners):
    held, aux, width, _ = blocks.shape
    rows = aux * width
    return pl.pallas_call(
        pick_kernel,
        out_shape=jax.ShapeDtypeStruct((owners, CAP * rows + NOTE, width), blocks.dtype),
        in_specs=[
            pl.BlockSpec(memory_space=pltpu.SMEM),
            pl.BlockSpec(memory_space=pltpu.VMEM),
        ],
        out_specs=pl.BlockSpec(memory_space=pltpu.VMEM),
        scratch_shapes=[
            pltpu.SMEM((owners,), jnp.int32),
            pltpu.SMEM((owners, CAP), jnp.int32),
        ],
        compiler_params=pltpu.CompilerParams(vmem_limit_bytes=16 * 1024 * 1024),
        cost_estimate=pl.CostEstimate(flops=0, bytes_accessed=4 * blocks.size, transcendentals=0),
        name="pick",
    )(pairs, blocks.reshape(held, rows, width))


def place_kernel(first_ref, *refs):
    slot_refs, out_ref, total = refs[:CAP], refs[CAP], refs[CAP + 1]
    width = total.shape[1]
    total[...] = jnp.zeros_like(total)

    def body(s, carry):
        for k, slots in enumerate(slot_refs):
            m = first_ref[s * CAP + k]

            @pl.when(m >= 0)
            def _():
                rows = pl.ds(pl.multiple_of(m * width, width), width)
                total[rows, :] += slots[s].astype(jnp.float32)

        return carry

    lax.fori_loop(0, slot_refs[0].shape[0], body, 0)
    out_ref[...] = total[...].astype(out_ref.dtype)


def place(first, recv, start, depth, aux, rows):
    senders, _, width = recv.shape

    def slot(k):
        return pl.BlockSpec((senders, width, width), lambda p, first: (0, k * aux + start + p, 0))

    size = senders * CAP * depth * width * width
    return pl.pallas_call(
        place_kernel,
        out_shape=jax.ShapeDtypeStruct((rows, depth * width), recv.dtype),
        grid_spec=pltpu.PrefetchScalarGridSpec(
            num_scalar_prefetch=1,
            grid=(depth,),
            in_specs=[slot(k) for k in range(CAP)],
            out_specs=pl.BlockSpec((rows, width), lambda p, first: (0, p)),
            scratch_shapes=[pltpu.VMEM((rows, width), jnp.float32)],
        ),
        compiler_params=pltpu.CompilerParams(vmem_limit_bytes=8 * 1024 * 1024),
        cost_estimate=pl.CostEstimate(flops=size, bytes_accessed=4 * size, transcendentals=0),
        name="place",
    )(first, *[recv] * CAP)


FROM = (0, -1, 1, 2)


def hop(x, by, first):
    pairs = []
    for device in range(128):
        xl, y, xh, core = device // 16 % 2, device // 4 % 4, device // 2 % 2, device % 2
        if (core == 0) == first:
            to = device + ((y + by) % 4 - y) * 4
        else:
            to_x = (2 * xh + xl + by) % 4
            to = device + (to_x % 2 - xl) * 16 + (to_x // 2 - xh) * 2
        pairs.append((device, to))
    return lax.ppermute(x, AXES, pairs)


def ring(x, first):
    return jnp.concatenate([x] + [hop(x, by, first) for by in (1, -1, 2)], axis=0)


def lay_kernel(spots, *refs):
    pieces, out_ref = refs[:-1], refs[-1]
    z, y, core = lax.axis_index("z"), lax.axis_index("y"), lax.axis_index("core")
    x = 2 * lax.axis_index("xh") + lax.axis_index("xl")
    for piece, (side, dz, start) in zip(pieces, spots, strict=True):
        source = (core + side) % 2
        for i in range(piece.shape[0]):
            late, early = FROM[(start + i) // 4], FROM[(start + i) % 4]
            to_x = (x + 4 + late + (early - late) * source) % 4
            to_y = (y + 4 + early + (late - early) * source) % 4
            out_ref[(z + 4 + dz) % 4, to_x % 2, to_y, to_x // 2, source] = piece[i]


def lay(spots, pieces):
    _, rows, columns = pieces[0].shape
    out = pl.pallas_call(
        functools.partial(lay_kernel, spots),
        out_shape=jax.ShapeDtypeStruct((*SIZES, rows, columns), pieces[0].dtype),
        in_specs=[pl.BlockSpec(memory_space=pltpu.VMEM)] * len(pieces),
        out_specs=pl.BlockSpec(memory_space=pltpu.VMEM),
        compiler_params=pltpu.CompilerParams(vmem_limit_bytes=20 * 1024 * 1024),
        cost_estimate=pl.CostEstimate(
            flops=0, bytes_accessed=512 * rows * columns, transcendentals=0
        ),
        name="lay",
    )(*pieces)
    return out.reshape(-1, columns)


def z_near(mine):
    return up(mine), down(mine)


def z_far(mine, near):
    half = mine.shape[0] // 2
    return up(near[0][:half]), down(near[1][half:])


def assemble(mine, near, far):
    pieces = [mine, *near, *far]
    spots = [(0, 0), (-1, 0), (1, 0), (2, 0), (2, mine.shape[0] // 2)]
    spots = [(side, dz, start) for side in range(2) for dz, start in spots]
    return lay(spots, pieces + [other_core(p) for p in pieces])


def pair_kernel(x_ref, *refs):
    y_refs, out_ref = refs[:-1], refs[-1]
    blocks, width, _ = x_ref.shape
    aux_x = x_ref.shape[2] // width
    same = lax.broadcasted_iota(jnp.int32, (width, width), 0) == lax.broadcasted_iota(
        jnp.int32, (width, width), 1
    )
    x = jnp.concatenate(
        [
            jnp.concatenate(
                [x_ref[k, :, p * width : (p + 1) * width] for k in range(blocks)], axis=1
            )
            for p in range(aux_x)
        ],
        axis=0,
    )
    done = 0
    for y_ref in y_refs:
        products = lax.dot_general(
            x, y_ref[...], (((1,), (1,)), ((), ())), preferred_element_type=jnp.float32
        )
        aux_y = y_ref.shape[0] // width
        for q in range(aux_y):
            for p in range(aux_x):
                tile = products[p * width : (p + 1) * width, q * width : (q + 1) * width]
                tile = jnp.where(same, tile, 0.0).reshape(width // 8, 8, width)
                out_ref[(done + q) * aux_x + p] = tile.sum(axis=0)
        done += aux_y


def pair_sums(x, ys):
    _, width, _ = x.shape
    aux_x, aux_y = x.shape[2] // width, sum(y.shape[0] for y in ys) // width
    sums = pl.pallas_call(
        pair_kernel,
        out_shape=jax.ShapeDtypeStruct((aux_y * aux_x, 8, width), jnp.float32),
        in_specs=[pl.BlockSpec(memory_space=pltpu.VMEM)] * (1 + len(ys)),
        out_specs=pl.BlockSpec(memory_space=pltpu.VMEM),
        compiler_params=pltpu.CompilerParams(vmem_limit_bytes=16 * 1024 * 1024),
        cost_estimate=pl.CostEstimate(
            flops=2 * x.size * aux_y, bytes_accessed=6 * x.size, transcendentals=0
        ),
        name="pair",
    )(x, *ys)
    return sums.sum(axis=(1, 2)).reshape(aux_y, aux_x).T


def col_sum(x):
    x = x + other_core(x)
    x = x + permute(x, "xh", lambda k: 1 - k)
    x = x + permute(x, "y", lambda k: k ^ 1)
    return x + permute(x, "y", lambda k: k ^ 2)


def shards(tensor_blocks, block_list, occ_green, virt_green):
    col_count = lax.axis_size(COL)
    blocks = tensor_blocks[0]
    aux, width = blocks.shape[1], blocks.shape[-1]
    basis_total = occ_green.shape[1]
    shard_rows = occ_green.shape[0]

    picked = pick(block_list[0], blocks, col_count)
    line = ring(jnp.concatenate([occ_green, virt_green.T], axis=0)[None], True)
    plane = ring(line, False)
    picked, plane = lax.optimization_barrier((picked, plane))
    recv = lax.all_to_all(picked, COL, split_axis=0, concat_axis=0, tiled=True)
    notes = CAP * aux * width
    recv_first = recv[:, notes : notes + CAP, 0].astype(jnp.int32).reshape(-1) - 1

    occ_plane, virt_plane = plane[:, :shard_rows], plane[:, shard_rows:]
    occ_near = z_near(occ_plane)
    occ_far = z_far(occ_plane, occ_near)
    occ_far, virt_plane = lax.optimization_barrier((occ_far, virt_plane))
    virt_near = z_near(virt_plane)
    virt_far = z_far(virt_plane, virt_near)
    occ = assemble(occ_plane, occ_near, occ_far)
    virt_t = assemble(virt_plane, virt_near, virt_far)

    dense, turned, start = [], [], 0
    for depth in CHUNKS:
        dense.append(place(recv_first, recv, start, depth, aux, basis_total))
        half = jnp.dot(occ, dense[-1], preferred_element_type=jnp.float32).astype(jnp.bfloat16)
        half = half.reshape(col_count, width, -1)
        turned.append(lax.all_to_all(half, COL, split_axis=0, concat_axis=0, tiled=True))
        start += depth

    virt_half = [
        lax.dot_general(
            d, virt_t, (((0,), (0,)), ((), ())), preferred_element_type=jnp.float32
        ).astype(jnp.bfloat16)
        for d in dense
    ]
    sums = jnp.concatenate([pair_sums(x, virt_half) for x in turned], axis=0)
    return (col_sum(sums) / float(basis_total))[None]


def solution(mesh):
    fine = Mesh(mesh.devices.reshape(SIZES), AXES)
    in_specs = (
        P(ROW, COL, None, None, None),
        P(ROW, COL, None),
        P(ROW + COL, None),
        P(None, ROW + COL),
    )
    return jax.shard_map(
        shards, mesh=fine, in_specs=in_specs, out_specs=P(ROW, None, None), check_vma=False
    )
```

```python
import functools

import jax
import jax.numpy as jnp
from jax import lax
from jax.experimental import pallas as pl
from jax.experimental.pallas import tpu as pltpu
from jax.sharding import Mesh
from jax.sharding import PartitionSpec as P

CAP = 2
CHUNKS = (3, 3)
NOTE = 16
AXES = ("z", "xl", "y", "xh", "core")
SIZES = (4, 2, 4, 2, 2)
COL = ("y", "xh", "core")
ROW = ("z", "xl")


def moved(axis, to):
    where = AXES.index(axis)
    stride = 1
    for size in SIZES[where + 1 :]:
        stride *= size
    total = 1
    for size in SIZES:
        total *= size
    pairs = []
    for device in range(total):
        k = device // stride % SIZES[where]
        pairs.append((device, device + (to(k) - k) * stride))
    return pairs


def permute(x, axis, to):
    return lax.ppermute(x, AXES, moved(axis, to))


def up(x, by=1):
    return permute(x, "z", lambda k: (k + by) % 4)


def down(x):
    return permute(x, "z", lambda k: (k - 1) % 4)


def other_core(x):
    return permute(x, "core", lambda k: 1 - k)


def pick_kernel(pairs_ref, blocks_ref, out_ref, count, first):
    held, rows, width = blocks_ref.shape
    owners = count.shape[0]
    for d in range(owners):
        count[d] = 0
        for k in range(CAP):
            first[d, k] = 0

    def body(t, carry):
        l = pairs_ref[t, 1]
        k = count[l]
        count[l] = k + 1
        first[l, k] = pairs_ref[t, 0] + 1
        out_ref[l, pl.ds(pl.multiple_of(k * rows, rows), rows), :] = blocks_ref[t]
        return carry

    lax.fori_loop(0, held, body, 0)
    which = lax.broadcasted_iota(jnp.int32, (NOTE, width), 0)
    for d in range(owners):
        note = jnp.zeros((NOTE, width), jnp.float32)
        for k in range(CAP):
            note = jnp.where(which == k, first[d, k].astype(jnp.float32), note)
        out_ref[d, CAP * rows :, :] = note.astype(out_ref.dtype)


def pick(pairs, blocks, owners):
    held, aux, width, _ = blocks.shape
    rows = aux * width
    return pl.pallas_call(
        pick_kernel,
        out_shape=jax.ShapeDtypeStruct((owners, CAP * rows + NOTE, width), blocks.dtype),
        in_specs=[
            pl.BlockSpec(memory_space=pltpu.SMEM),
            pl.BlockSpec(memory_space=pltpu.VMEM),
        ],
        out_specs=pl.BlockSpec(memory_space=pltpu.VMEM),
        scratch_shapes=[
            pltpu.SMEM((owners,), jnp.int32),
            pltpu.SMEM((owners, CAP), jnp.int32),
        ],
        compiler_params=pltpu.CompilerParams(vmem_limit_bytes=16 * 1024 * 1024),
        cost_estimate=pl.CostEstimate(flops=0, bytes_accessed=4 * blocks.size, transcendentals=0),
        name="pick",
    )(pairs, blocks.reshape(held, rows, width))


def place_kernel(first_ref, *refs):
    slot_refs, out_ref, total = refs[:CAP], refs[CAP], refs[CAP + 1]
    width = total.shape[1]
    total[...] = jnp.zeros_like(total)

    def body(s, carry):
        for k, slots in enumerate(slot_refs):
            m = first_ref[s * CAP + k]

            @pl.when(m >= 0)
            def _():
                rows = pl.ds(pl.multiple_of(m * width, width), width)
                total[rows, :] += slots[s].astype(jnp.float32)

        return carry

    lax.fori_loop(0, slot_refs[0].shape[0], body, 0)
    out_ref[...] = total[...].astype(out_ref.dtype)


def place(first, recv, start, depth, aux, rows):
    senders, _, width = recv.shape

    def slot(k):
        return pl.BlockSpec((senders, width, width), lambda p, first: (0, k * aux + start + p, 0))

    size = senders * CAP * depth * width * width
    return pl.pallas_call(
        place_kernel,
        out_shape=jax.ShapeDtypeStruct((rows, depth * width), recv.dtype),
        grid_spec=pltpu.PrefetchScalarGridSpec(
            num_scalar_prefetch=1,
            grid=(depth,),
            in_specs=[slot(k) for k in range(CAP)],
            out_specs=pl.BlockSpec((rows, width), lambda p, first: (0, p)),
            scratch_shapes=[pltpu.VMEM((rows, width), jnp.float32)],
        ),
        compiler_params=pltpu.CompilerParams(vmem_limit_bytes=8 * 1024 * 1024),
        cost_estimate=pl.CostEstimate(flops=size, bytes_accessed=4 * size, transcendentals=0),
        name="place",
    )(first, *[recv] * CAP)


FROM = (0, -1, 1, 2)


def hop(x, by, first):
    pairs = []
    for device in range(128):
        xl, y, xh, core = device // 16 % 2, device // 4 % 4, device // 2 % 2, device % 2
        if (core == 0) == first:
            to = device + ((y + by) % 4 - y) * 4
        else:
            to_x = (2 * xh + xl + by) % 4
            to = device + (to_x % 2 - xl) * 16 + (to_x // 2 - xh) * 2
        pairs.append((device, to))
    return lax.ppermute(x, AXES, pairs)


def ring(x, first):
    return [x] + [hop(x, by, first) for by in (1, -1, 2)]


def lay_kernel(spots, *refs):
    pieces, out_ref = refs[:-1], refs[-1]
    z, y, core = lax.axis_index("z"), lax.axis_index("y"), lax.axis_index("core")
    x = 2 * lax.axis_index("xh") + lax.axis_index("xl")
    for piece, (side, dz, start) in zip(pieces, spots, strict=True):
        source = (core + side) % 2
        for i in range(piece.shape[0]):
            late, early = FROM[(start + i) // 4], FROM[(start + i) % 4]
            to_x = (x + 4 + late + (early - late) * source) % 4
            to_y = (y + 4 + early + (late - early) * source) % 4
            out_ref[(z + 4 + dz) % 4, to_x % 2, to_y, to_x // 2, source] = piece[i]


def lay(spots, pieces):
    _, rows, columns = pieces[0].shape
    out = pl.pallas_call(
        functools.partial(lay_kernel, spots),
        out_shape=jax.ShapeDtypeStruct((*SIZES, rows, columns), pieces[0].dtype),
        in_specs=[pl.BlockSpec(memory_space=pltpu.VMEM)] * len(pieces),
        out_specs=pl.BlockSpec(memory_space=pltpu.VMEM),
        compiler_params=pltpu.CompilerParams(vmem_limit_bytes=20 * 1024 * 1024),
        cost_estimate=pl.CostEstimate(
            flops=0, bytes_accessed=512 * rows * columns, transcendentals=0
        ),
        name="lay",
    )(*pieces)
    return out.reshape(-1, columns)


FORWARDED = ((0, 0), (-1, 0), (1, 0), (2, 0), (2, 8))
DIRECT = ((0, 0), (-1, 0), (1, 0), (2, 0))


def z_forwarded(mine):
    half = mine.shape[0] // 2
    below, above = up(mine), down(mine)
    return [mine, below, above, up(below[:half]), down(above[half:])]


def z_direct(mine):
    return [mine, up(mine), down(mine), up(mine, 2)]


def assemble(spots, pieces):
    spots = [(side, *spot) for side in range(2) for spot in spots]
    return lay(spots, pieces + [other_core(piece) for piece in pieces])


def pair_kernel(x_ref, *refs):
    y_refs, out_ref = refs[:-1], refs[-1]
    blocks, width, _ = x_ref.shape
    aux_x = x_ref.shape[2] // width
    same = lax.broadcasted_iota(jnp.int32, (width, width), 0) == lax.broadcasted_iota(
        jnp.int32, (width, width), 1
    )
    x = jnp.concatenate(
        [
            jnp.concatenate(
                [x_ref[k, :, p * width : (p + 1) * width] for k in range(blocks)], axis=1
            )
            for p in range(aux_x)
        ],
        axis=0,
    )
    done = 0
    for y_ref in y_refs:
        products = lax.dot_general(
            x, y_ref[...], (((1,), (1,)), ((), ())), preferred_element_type=jnp.float32
        )
        aux_y = y_ref.shape[0] // width
        for q in range(aux_y):
            for p in range(aux_x):
                tile = products[p * width : (p + 1) * width, q * width : (q + 1) * width]
                tile = jnp.where(same, tile, 0.0).reshape(width // 8, 8, width)
                out_ref[(done + q) * aux_x + p] = tile.sum(axis=0)
        done += aux_y


def pair_sums(x, ys):
    _, width, _ = x.shape
    aux_x, aux_y = x.shape[2] // width, sum(y.shape[0] for y in ys) // width
    sums = pl.pallas_call(
        pair_kernel,
        out_shape=jax.ShapeDtypeStruct((aux_y * aux_x, 8, width), jnp.float32),
        in_specs=[pl.BlockSpec(memory_space=pltpu.VMEM)] * (1 + len(ys)),
        out_specs=pl.BlockSpec(memory_space=pltpu.VMEM),
        compiler_params=pltpu.CompilerParams(vmem_limit_bytes=16 * 1024 * 1024),
        cost_estimate=pl.CostEstimate(
            flops=2 * x.size * aux_y, bytes_accessed=6 * x.size, transcendentals=0
        ),
        name="pair",
    )(x, *ys)
    return sums.sum(axis=(1, 2)).reshape(aux_y, aux_x).T


def col_sum(x):
    x = x + other_core(x)
    x = x + permute(x, "xh", lambda k: 1 - k)
    x = x + permute(x, "y", lambda k: k ^ 1)
    return x + permute(x, "y", lambda k: k ^ 2)


def shards(tensor_blocks, block_list, occ_green, virt_green):
    col_count = lax.axis_size(COL)
    blocks = tensor_blocks[0]
    aux, width = blocks.shape[1], blocks.shape[-1]
    basis_total = occ_green.shape[1]
    shard_rows = occ_green.shape[0]

    picked = pick(block_list[0], blocks, col_count)
    line = ring(jnp.concatenate([occ_green, virt_green.T], axis=0)[None], True)
    plane = ring(jnp.concatenate(line, axis=0), False)
    picked, plane = lax.optimization_barrier((picked, plane))
    plane = jnp.concatenate(plane, axis=0)
    recv = lax.all_to_all(picked, COL, split_axis=0, concat_axis=0, tiled=True)
    notes = CAP * aux * width
    recv_first = recv[:, notes : notes + CAP, 0].astype(jnp.int32).reshape(-1) - 1

    occ_plane, virt_plane = plane[:, :shard_rows], plane[:, shard_rows:]
    occ_pieces = z_forwarded(occ_plane)
    occ_pieces, virt_plane = lax.optimization_barrier((occ_pieces, virt_plane))
    virt_pieces = z_direct(virt_plane)
    occ = assemble(FORWARDED, occ_pieces)

    dense, turned, start = [], [], 0
    for depth in CHUNKS:
        dense.append(place(recv_first, recv, start, depth, aux, basis_total))
        half = jnp.dot(occ, dense[-1], preferred_element_type=jnp.float32).astype(jnp.bfloat16)
        if start == 0:
            _, virt_pieces = lax.optimization_barrier((half, virt_pieces))
        half = half.reshape(col_count, width, -1)
        turned.append(lax.all_to_all(half, COL, split_axis=0, concat_axis=0, tiled=True))
        start += depth

    virt_t = assemble(DIRECT, virt_pieces)
    virt_half = [
        lax.dot_general(
            d, virt_t, (((0,), (0,)), ((), ())), preferred_element_type=jnp.float32
        ).astype(jnp.bfloat16)
        for d in dense
    ]
    sums = jnp.concatenate([pair_sums(x, virt_half) for x in turned], axis=0)
    return (col_sum(sums) / float(basis_total))[None]


def solution(mesh):
    fine = Mesh(mesh.devices.reshape(SIZES), AXES)
    in_specs = (
        P(ROW, COL, None, None, None),
        P(ROW, COL, None),
        P(ROW + COL, None),
        P(None, ROW + COL),
    )
    return jax.shard_map(
        shards, mesh=fine, in_specs=in_specs, out_specs=P(ROW, None, None), check_vma=False
    )
```

```python
import functools

import jax
import jax.numpy as jnp
from jax import lax
from jax.experimental import pallas as pl
from jax.experimental.pallas import tpu as pltpu
from jax.sharding import Mesh
from jax.sharding import PartitionSpec as P

CAP = 2
CHUNKS = (3, 3)
NOTE = 16
AXES = ("z", "xl", "y", "xh", "core")
SIZES = (4, 2, 4, 2, 2)
COL = ("y", "xh", "core")
ROW = ("z", "xl")


def moved(axis, to):
    where = AXES.index(axis)
    stride = 1
    for size in SIZES[where + 1 :]:
        stride *= size
    total = 1
    for size in SIZES:
        total *= size
    pairs = []
    for device in range(total):
        k = device // stride % SIZES[where]
        pairs.append((device, device + (to(k) - k) * stride))
    return pairs


def permute(x, axis, to):
    return lax.ppermute(x, AXES, moved(axis, to))


def up(x, by=1):
    return permute(x, "z", lambda k: (k + by) % 4)


def down(x):
    return permute(x, "z", lambda k: (k - 1) % 4)


def other_core(x):
    return permute(x, "core", lambda k: 1 - k)


def pick_kernel(pairs_ref, blocks_ref, out_ref, count, first):
    held, rows, width = blocks_ref.shape
    owners = count.shape[0]
    for d in range(owners):
        count[d] = 0
        for k in range(CAP):
            first[d, k] = 0

    def body(t, carry):
        l = pairs_ref[t, 1]
        k = count[l]
        count[l] = k + 1
        first[l, k] = pairs_ref[t, 0] + 1
        out_ref[l, pl.ds(pl.multiple_of(k * rows, rows), rows), :] = blocks_ref[t]
        return carry

    lax.fori_loop(0, held, body, 0)
    which = lax.broadcasted_iota(jnp.int32, (NOTE, width), 0)
    for d in range(owners):
        note = jnp.zeros((NOTE, width), jnp.float32)
        for k in range(CAP):
            note = jnp.where(which == k, first[d, k].astype(jnp.float32), note)
        out_ref[d, CAP * rows :, :] = note.astype(out_ref.dtype)


def pick(pairs, blocks, owners):
    held, aux, width, _ = blocks.shape
    rows = aux * width
    return pl.pallas_call(
        pick_kernel,
        out_shape=jax.ShapeDtypeStruct((owners, CAP * rows + NOTE, width), blocks.dtype),
        in_specs=[
            pl.BlockSpec(memory_space=pltpu.SMEM),
            pl.BlockSpec(memory_space=pltpu.VMEM),
        ],
        out_specs=pl.BlockSpec(memory_space=pltpu.VMEM),
        scratch_shapes=[
            pltpu.SMEM((owners,), jnp.int32),
            pltpu.SMEM((owners, CAP), jnp.int32),
        ],
        compiler_params=pltpu.CompilerParams(vmem_limit_bytes=16 * 1024 * 1024),
        cost_estimate=pl.CostEstimate(flops=0, bytes_accessed=4 * blocks.size, transcendentals=0),
        name="pick",
    )(pairs, blocks.reshape(held, rows, width))


def place_kernel(first_ref, *refs):
    slot_refs, out_ref, total = refs[:CAP], refs[CAP], refs[CAP + 1]
    width = total.shape[1]
    total[...] = jnp.zeros_like(total)

    def body(s, carry):
        for k, slots in enumerate(slot_refs):
            m = first_ref[s * CAP + k]

            @pl.when(m >= 0)
            def _():
                rows = pl.ds(pl.multiple_of(m * width, width), width)
                total[rows, :] += slots[s].astype(jnp.float32)

        return carry

    lax.fori_loop(0, slot_refs[0].shape[0], body, 0)
    out_ref[...] = total[...].astype(out_ref.dtype)


def place(first, recv, start, depth, aux, rows):
    senders, _, width = recv.shape

    def slot(k):
        return pl.BlockSpec((senders, width, width), lambda p, first: (0, k * aux + start + p, 0))

    size = senders * CAP * depth * width * width
    return pl.pallas_call(
        place_kernel,
        out_shape=jax.ShapeDtypeStruct((rows, depth * width), recv.dtype),
        grid_spec=pltpu.PrefetchScalarGridSpec(
            num_scalar_prefetch=1,
            grid=(depth,),
            in_specs=[slot(k) for k in range(CAP)],
            out_specs=pl.BlockSpec((rows, width), lambda p, first: (0, p)),
            scratch_shapes=[pltpu.VMEM((rows, width), jnp.float32)],
        ),
        compiler_params=pltpu.CompilerParams(vmem_limit_bytes=8 * 1024 * 1024),
        cost_estimate=pl.CostEstimate(flops=size, bytes_accessed=4 * size, transcendentals=0),
        name="place",
    )(first, *[recv] * CAP)


FROM = (0, -1, 1, 2)


def hop(x, by, first):
    pairs = []
    for device in range(128):
        xl, y, xh, core = device // 16 % 2, device // 4 % 4, device // 2 % 2, device % 2
        if (core == 0) == first:
            to = device + ((y + by) % 4 - y) * 4
        else:
            to_x = (2 * xh + xl + by) % 4
            to = device + (to_x % 2 - xl) * 16 + (to_x // 2 - xh) * 2
        pairs.append((device, to))
    return lax.ppermute(x, AXES, pairs)


def ring(x, first):
    return [x] + [hop(x, by, first) for by in (1, -1, 2)]


def lay_kernel(spots, *refs):
    pieces, out_ref = refs[:-1], refs[-1]
    z, y, core = lax.axis_index("z"), lax.axis_index("y"), lax.axis_index("core")
    x = 2 * lax.axis_index("xh") + lax.axis_index("xl")
    for piece, (side, dz, start) in zip(pieces, spots, strict=True):
        source = (core + side) % 2
        for i in range(piece.shape[0]):
            late, early = FROM[(start + i) // 4], FROM[(start + i) % 4]
            to_x = (x + 4 + late + (early - late) * source) % 4
            to_y = (y + 4 + early + (late - early) * source) % 4
            out_ref[(z + 4 + dz) % 4, to_x % 2, to_y, to_x // 2, source] = piece[i]


def lay(spots, pieces):
    _, rows, columns = pieces[0].shape
    out = pl.pallas_call(
        functools.partial(lay_kernel, spots),
        out_shape=jax.ShapeDtypeStruct((*SIZES, rows, columns), pieces[0].dtype),
        in_specs=[pl.BlockSpec(memory_space=pltpu.VMEM)] * len(pieces),
        out_specs=pl.BlockSpec(memory_space=pltpu.VMEM),
        compiler_params=pltpu.CompilerParams(vmem_limit_bytes=20 * 1024 * 1024),
        cost_estimate=pl.CostEstimate(
            flops=0, bytes_accessed=512 * rows * columns, transcendentals=0
        ),
        name="lay",
    )(*pieces)
    return out.reshape(-1, columns)


FORWARDED = ((0, 0), (-1, 0), (1, 0), (2, 0), (2, 8))
DIRECT = ((0, 0), (-1, 0), (1, 0), (2, 0))


def z_forwarded(mine):
    half = mine.shape[0] // 2
    below, above = up(mine), down(mine)
    return [mine, below, above, up(below[:half]), down(above[half:])]


def z_direct(mine):
    return [mine, up(mine), down(mine), up(mine, 2)]


def assemble(spots, pieces, copies):
    spots = [(side, *spot) for side in range(2) for spot in spots]
    return lay(spots, pieces + copies)


def pair_kernel(x_ref, *refs):
    y_refs, out_ref = refs[:-1], refs[-1]
    blocks, width, _ = x_ref.shape
    aux_x = x_ref.shape[2] // width
    same = lax.broadcasted_iota(jnp.int32, (width, width), 0) == lax.broadcasted_iota(
        jnp.int32, (width, width), 1
    )
    x = jnp.concatenate(
        [
            jnp.concatenate(
                [x_ref[k, :, p * width : (p + 1) * width] for k in range(blocks)], axis=1
            )
            for p in range(aux_x)
        ],
        axis=0,
    )
    done = 0
    for y_ref in y_refs:
        products = lax.dot_general(
            x, y_ref[...], (((1,), (1,)), ((), ())), preferred_element_type=jnp.float32
        )
        aux_y = y_ref.shape[0] // width
        for q in range(aux_y):
            for p in range(aux_x):
                tile = products[p * width : (p + 1) * width, q * width : (q + 1) * width]
                tile = jnp.where(same, tile, 0.0).reshape(width // 8, 8, width)
                out_ref[(done + q) * aux_x + p] = tile.sum(axis=0)
        done += aux_y


def pair_sums(x, ys):
    _, width, _ = x.shape
    aux_x, aux_y = x.shape[2] // width, sum(y.shape[0] for y in ys) // width
    sums = pl.pallas_call(
        pair_kernel,
        out_shape=jax.ShapeDtypeStruct((aux_y * aux_x, 8, width), jnp.float32),
        in_specs=[pl.BlockSpec(memory_space=pltpu.VMEM)] * (1 + len(ys)),
        out_specs=pl.BlockSpec(memory_space=pltpu.VMEM),
        compiler_params=pltpu.CompilerParams(vmem_limit_bytes=16 * 1024 * 1024),
        cost_estimate=pl.CostEstimate(
            flops=2 * x.size * aux_y, bytes_accessed=6 * x.size, transcendentals=0
        ),
        name="pair",
    )(x, *ys)
    return sums.sum(axis=(1, 2)).reshape(aux_y, aux_x).T


def col_sum(x):
    x = x + other_core(x)
    x = x + permute(x, "xh", lambda k: 1 - k)
    x = x + permute(x, "y", lambda k: k ^ 1)
    return x + permute(x, "y", lambda k: k ^ 2)


def shards(tensor_blocks, block_list, occ_green, virt_green):
    col_count = lax.axis_size(COL)
    blocks = tensor_blocks[0]
    aux, width = blocks.shape[1], blocks.shape[-1]
    basis_total = occ_green.shape[1]
    shard_rows = occ_green.shape[0]

    picked = pick(block_list[0], blocks, col_count)
    line = ring(jnp.concatenate([occ_green, virt_green.T], axis=0)[None], True)
    plane = ring(jnp.concatenate(line, axis=0), False)
    picked, plane = lax.optimization_barrier((picked, plane))
    plane = jnp.concatenate(plane, axis=0)
    recv = lax.all_to_all(picked, COL, split_axis=0, concat_axis=0, tiled=True)
    notes = CAP * aux * width
    recv_first = recv[:, notes : notes + CAP, 0].astype(jnp.int32).reshape(-1) - 1

    occ_plane, virt_plane = plane[:, :shard_rows], plane[:, shard_rows:]
    occ_pieces = z_forwarded(occ_plane)
    occ_pieces, virt_plane = lax.optimization_barrier((occ_pieces, virt_plane))
    virt_pieces = z_direct(virt_plane)
    occ = assemble(FORWARDED, occ_pieces, [other_core(p) for p in occ_pieces])

    dense, turned, start = [], [], 0
    for depth in CHUNKS:
        dense.append(place(recv_first, recv, start, depth, aux, basis_total))
        half = jnp.dot(occ, dense[-1], preferred_element_type=jnp.float32).astype(jnp.bfloat16)
        cut = half.reshape(col_count, width, -1)
        turned.append(lax.all_to_all(cut, COL, split_axis=0, concat_axis=0, tiled=True))
        start += depth

    _, virt_pieces = lax.optimization_barrier((half, virt_pieces))
    virt_copies = [other_core(p) for p in virt_pieces]
    turned[0], virt_copies = lax.optimization_barrier((turned[0], virt_copies))
    virt_t = assemble(DIRECT, virt_pieces, virt_copies)
    virt_half = [
        lax.dot_general(
            d, virt_t, (((0,), (0,)), ((), ())), preferred_element_type=jnp.float32
        ).astype(jnp.bfloat16)
        for d in dense
    ]
    sums = jnp.concatenate([pair_sums(x, virt_half) for x in turned], axis=0)
    return (col_sum(sums) / float(basis_total))[None]


def solution(mesh):
    fine = Mesh(mesh.devices.reshape(SIZES), AXES)
    in_specs = (
        P(ROW, COL, None, None, None),
        P(ROW, COL, None),
        P(ROW + COL, None),
        P(None, ROW + COL),
    )
    return jax.shard_map(
        shards, mesh=fine, in_specs=in_specs, out_specs=P(ROW, None, None), check_vma=False
    )
```

```python
import functools

import jax
import jax.numpy as jnp
from jax import lax
from jax.experimental import pallas as pl
from jax.experimental.pallas import tpu as pltpu
from jax.sharding import Mesh
from jax.sharding import PartitionSpec as P

CAP = 2
CHUNKS = (3, 3)
NOTE = 16
AXES = ("z", "xl", "y", "xh", "core")
SIZES = (4, 2, 4, 2, 2)
COL = ("y", "xh", "core")
ROW = ("z", "xl")


def moved(axis, to):
    where = AXES.index(axis)
    stride = 1
    for size in SIZES[where + 1 :]:
        stride *= size
    total = 1
    for size in SIZES:
        total *= size
    pairs = []
    for device in range(total):
        k = device // stride % SIZES[where]
        pairs.append((device, device + (to(k) - k) * stride))
    return pairs


def permute(x, axis, to):
    return lax.ppermute(x, AXES, moved(axis, to))


def up(x, by=1):
    return permute(x, "z", lambda k: (k + by) % 4)


def down(x):
    return permute(x, "z", lambda k: (k - 1) % 4)


def other_core(x):
    return permute(x, "core", lambda k: 1 - k)


def pick_kernel(pairs_ref, blocks_ref, out_ref, count, first):
    held, rows, width = blocks_ref.shape
    owners = count.shape[0]
    for d in range(owners):
        count[d] = 0
        for k in range(CAP):
            first[d, k] = 0

    def body(t, carry):
        l = pairs_ref[t, 1]
        k = count[l]
        count[l] = k + 1
        first[l, k] = pairs_ref[t, 0] + 1
        out_ref[l, pl.ds(pl.multiple_of(k * rows, rows), rows), :] = blocks_ref[t]
        return carry

    lax.fori_loop(0, held, body, 0)
    which = lax.broadcasted_iota(jnp.int32, (NOTE, width), 0)
    for d in range(owners):
        note = jnp.zeros((NOTE, width), jnp.float32)
        for k in range(CAP):
            note = jnp.where(which == k, first[d, k].astype(jnp.float32), note)
        out_ref[d, CAP * rows :, :] = note.astype(out_ref.dtype)


def pick(pairs, blocks, owners):
    held, aux, width, _ = blocks.shape
    rows = aux * width
    return pl.pallas_call(
        pick_kernel,
        out_shape=jax.ShapeDtypeStruct((owners, CAP * rows + NOTE, width), blocks.dtype),
        in_specs=[
            pl.BlockSpec(memory_space=pltpu.SMEM),
            pl.BlockSpec(memory_space=pltpu.VMEM),
        ],
        out_specs=pl.BlockSpec(memory_space=pltpu.VMEM),
        scratch_shapes=[
            pltpu.SMEM((owners,), jnp.int32),
            pltpu.SMEM((owners, CAP), jnp.int32),
        ],
        compiler_params=pltpu.CompilerParams(vmem_limit_bytes=16 * 1024 * 1024),
        cost_estimate=pl.CostEstimate(flops=0, bytes_accessed=4 * blocks.size, transcendentals=0),
        name="pick",
    )(pairs, blocks.reshape(held, rows, width))


def place_kernel(first_ref, *refs):
    slot_refs, out_ref, total = refs[:CAP], refs[CAP], refs[CAP + 1]
    width = total.shape[1]
    total[...] = jnp.zeros_like(total)

    def body(s, carry):
        for k, slots in enumerate(slot_refs):
            m = first_ref[s * CAP + k]

            @pl.when(m >= 0)
            def _():
                rows = pl.ds(pl.multiple_of(m * width, width), width)
                total[rows, :] += slots[s].astype(jnp.float32)

        return carry

    lax.fori_loop(0, slot_refs[0].shape[0], body, 0)
    out_ref[...] = total[...].astype(out_ref.dtype)


def place(first, recv, start, depth, aux, rows):
    senders, _, width = recv.shape

    def slot(k):
        return pl.BlockSpec((senders, width, width), lambda p, first: (0, k * aux + start + p, 0))

    size = senders * CAP * depth * width * width
    return pl.pallas_call(
        place_kernel,
        out_shape=jax.ShapeDtypeStruct((rows, depth * width), recv.dtype),
        grid_spec=pltpu.PrefetchScalarGridSpec(
            num_scalar_prefetch=1,
            grid=(depth,),
            in_specs=[slot(k) for k in range(CAP)],
            out_specs=pl.BlockSpec((rows, width), lambda p, first: (0, p)),
            scratch_shapes=[pltpu.VMEM((rows, width), jnp.float32)],
        ),
        compiler_params=pltpu.CompilerParams(vmem_limit_bytes=8 * 1024 * 1024),
        cost_estimate=pl.CostEstimate(flops=size, bytes_accessed=4 * size, transcendentals=0),
        name="place",
    )(first, *[recv] * CAP)


FROM = (0, -1, 1, 2)


def hop(x, by, first):
    pairs = []
    for device in range(128):
        xl, y, xh, core = device // 16 % 2, device // 4 % 4, device // 2 % 2, device % 2
        if (core == 0) == first:
            to = device + ((y + by) % 4 - y) * 4
        else:
            to_x = (2 * xh + xl + by) % 4
            to = device + (to_x % 2 - xl) * 16 + (to_x // 2 - xh) * 2
        pairs.append((device, to))
    return lax.ppermute(x, AXES, pairs)


def ring(x, first):
    return [x] + [hop(x, by, first) for by in (1, -1, 2)]


def lay_kernel(spots, *refs):
    pieces, out_ref = refs[:-1], refs[-1]
    z, y, core = lax.axis_index("z"), lax.axis_index("y"), lax.axis_index("core")
    x = 2 * lax.axis_index("xh") + lax.axis_index("xl")
    for piece, (side, dz, start) in zip(pieces, spots, strict=True):
        source = (core + side) % 2
        for i in range(piece.shape[0]):
            late, early = FROM[(start + i) // 4], FROM[(start + i) % 4]
            to_x = (x + 4 + late + (early - late) * source) % 4
            to_y = (y + 4 + early + (late - early) * source) % 4
            out_ref[(z + 4 + dz) % 4, to_x % 2, to_y, to_x // 2, source] = piece[i]


def lay(spots, pieces):
    _, rows, columns = pieces[0].shape
    out = pl.pallas_call(
        functools.partial(lay_kernel, spots),
        out_shape=jax.ShapeDtypeStruct((*SIZES, rows, columns), pieces[0].dtype),
        in_specs=[pl.BlockSpec(memory_space=pltpu.VMEM)] * len(pieces),
        out_specs=pl.BlockSpec(memory_space=pltpu.VMEM),
        compiler_params=pltpu.CompilerParams(vmem_limit_bytes=20 * 1024 * 1024),
        cost_estimate=pl.CostEstimate(
            flops=0, bytes_accessed=512 * rows * columns, transcendentals=0
        ),
        name="lay",
    )(*pieces)
    return out.reshape(-1, columns)


FORWARDED = ((0, 0), (-1, 0), (1, 0), (2, 0), (2, 8))
DIRECT = ((0, 0), (-1, 0), (1, 0), (2, 0))


def z_forwarded(mine):
    half = mine.shape[0] // 2
    below, above = up(mine), down(mine)
    return [mine, below, above, up(below[:half]), down(above[half:])]


def z_direct(mine):
    return [mine, up(mine), down(mine), up(mine, 2)]


def assemble(spots, pieces, copies):
    spots = [(side, *spot) for side in range(2) for spot in spots]
    return lay(spots, pieces + copies)


def pair_kernel(x_ref, *refs):
    count = (len(refs) - 1) // 2
    y_refs, out_ref, totals = refs[:count], refs[count], refs[count + 1 :]
    blocks, width, _ = x_ref.shape
    aux_x = x_ref.shape[2] // width
    step = pl.program_id(0)
    x = jnp.concatenate(
        [
            jnp.concatenate(
                [x_ref[k, :, p * width : (p + 1) * width] for k in range(blocks)], axis=1
            )
            for p in range(aux_x)
        ],
        axis=0,
    )
    for y_ref, total in zip(y_refs, totals, strict=True):
        products = lax.dot_general(
            x, y_ref[...], (((1,), (1,)), ((), ())), preferred_element_type=jnp.float32
        )

        @pl.when(step == 0)
        def _():
            total[...] = products

        @pl.when(step > 0)
        def _():
            total[...] += products

    @pl.when(step == pl.num_programs(0) - 1)
    def _():
        same = lax.broadcasted_iota(jnp.int32, (width, width), 0) == lax.broadcasted_iota(
            jnp.int32, (width, width), 1
        )
        done = 0
        for total in totals:
            aux_y = total.shape[1] // width
            for q in range(aux_y):
                for p in range(aux_x):
                    tile = total[p * width : (p + 1) * width, q * width : (q + 1) * width]
                    tile = jnp.where(same, tile, 0.0).reshape(width // 8, 8, width)
                    out_ref[(done + q) * aux_x + p] = tile.sum(axis=0)
            done += aux_y


def pair_sums(x, ys):
    blocks, width, columns = x.shape
    aux_x, aux_y = columns // width, sum(y.shape[0] for y in ys) // width
    group = blocks // 4
    sums = pl.pallas_call(
        pair_kernel,
        out_shape=jax.ShapeDtypeStruct((aux_y * aux_x, 8, width), jnp.float32),
        grid=(4,),
        in_specs=[pl.BlockSpec((group, width, columns), lambda k: (k, 0, 0))]
        + [pl.BlockSpec((y.shape[0], group * width), lambda k: (0, k)) for y in ys],
        out_specs=pl.BlockSpec((aux_y * aux_x, 8, width), lambda k: (0, 0, 0)),
        scratch_shapes=[pltpu.VMEM((columns, y.shape[0]), jnp.float32) for y in ys],
        compiler_params=pltpu.CompilerParams(vmem_limit_bytes=60 * 1024 * 1024),
        cost_estimate=pl.CostEstimate(
            flops=2 * x.size * aux_y, bytes_accessed=6 * x.size, transcendentals=0
        ),
        name="pair",
    )(x, *ys)
    return sums.sum(axis=(1, 2)).reshape(aux_y, aux_x).T


def col_sum(x):
    x = x + other_core(x)
    x = x + permute(x, "xh", lambda k: 1 - k)
    x = x + permute(x, "y", lambda k: k ^ 1)
    return x + permute(x, "y", lambda k: 3 - k)


def shards(tensor_blocks, block_list, occ_green, virt_green):
    col_count = lax.axis_size(COL)
    blocks = tensor_blocks[0]
    aux, width = blocks.shape[1], blocks.shape[-1]
    basis_total = occ_green.shape[1]
    shard_rows = occ_green.shape[0]

    picked = pick(block_list[0], blocks, col_count)
    line = ring(jnp.concatenate([occ_green, virt_green.T], axis=0)[None], True)
    plane = ring(jnp.concatenate(line, axis=0), False)
    picked, plane = lax.optimization_barrier((picked, plane))
    plane = jnp.concatenate(plane, axis=0)
    recv = lax.all_to_all(picked, COL, split_axis=0, concat_axis=0, tiled=True)
    notes = CAP * aux * width
    recv_first = recv[:, notes : notes + CAP, 0].astype(jnp.int32).reshape(-1) - 1

    occ_plane, virt_plane = plane[:, :shard_rows], plane[:, shard_rows:]
    occ_pieces = z_forwarded(occ_plane)
    occ_pieces, virt_plane = lax.optimization_barrier((occ_pieces, virt_plane))
    virt_pieces = z_direct(virt_plane)
    occ = assemble(FORWARDED, occ_pieces, [other_core(p) for p in occ_pieces])

    dense, turned, start = [], [], 0
    for depth in CHUNKS:
        dense.append(place(recv_first, recv, start, depth, aux, basis_total))
        half = jnp.dot(occ, dense[-1], preferred_element_type=jnp.float32).astype(jnp.bfloat16)
        cut = half.reshape(col_count, width, -1)
        turned.append(lax.all_to_all(cut, COL, split_axis=0, concat_axis=0, tiled=True))
        recv_first, _ = lax.optimization_barrier((recv_first, half))
        start += depth

    _, virt_pieces = lax.optimization_barrier((half, virt_pieces))
    virt_copies = [other_core(p) for p in virt_pieces]
    turned[0], virt_copies = lax.optimization_barrier((turned[0], virt_copies))
    virt_t = assemble(DIRECT, virt_pieces, virt_copies)
    virt_half = [
        lax.dot_general(
            d, virt_t, (((0,), (0,)), ((), ())), preferred_element_type=jnp.float32
        ).astype(jnp.bfloat16)
        for d in dense
    ]
    sums = jnp.concatenate([pair_sums(x, virt_half) for x in turned], axis=0)
    return (col_sum(sums) / float(basis_total))[None]


def solution(mesh):
    fine = Mesh(mesh.devices.reshape(SIZES), AXES)
    in_specs = (
        P(ROW, COL, None, None, None),
        P(ROW, COL, None),
        P(ROW + COL, None),
        P(None, ROW + COL),
    )
    return jax.shard_map(
        shards, mesh=fine, in_specs=in_specs, out_specs=P(ROW, None, None), check_vma=False
    )
```

```python
import functools

import jax
import jax.numpy as jnp
from jax import lax
from jax.experimental import pallas as pl
from jax.experimental.pallas import tpu as pltpu
from jax.sharding import Mesh
from jax.sharding import PartitionSpec as P

CAP = 2
CHUNKS = (2, 4)
NOTE = 16
AXES = ("z", "xl", "y", "xh", "core")
SIZES = (4, 2, 4, 2, 2)
COL = ("y", "xh", "core")
ROW = ("z", "xl")


def moved(axis, to):
    where = AXES.index(axis)
    stride = 1
    for size in SIZES[where + 1 :]:
        stride *= size
    total = 1
    for size in SIZES:
        total *= size
    pairs = []
    for device in range(total):
        k = device // stride % SIZES[where]
        pairs.append((device, device + (to(k) - k) * stride))
    return pairs


def permute(x, axis, to):
    return lax.ppermute(x, AXES, moved(axis, to))


def up(x, by=1):
    return permute(x, "z", lambda k: (k + by) % 4)


def down(x):
    return permute(x, "z", lambda k: (k - 1) % 4)


def other_core(x):
    return permute(x, "core", lambda k: 1 - k)


def pick_kernel(pairs_ref, blocks_ref, out_ref, count, first):
    held, rows, width = blocks_ref.shape
    owners = count.shape[0]
    for d in range(owners):
        count[d] = 0
        for k in range(CAP):
            first[d, k] = 0

    def body(t, carry):
        l = pairs_ref[t, 1]
        k = count[l]
        count[l] = k + 1
        first[l, k] = pairs_ref[t, 0] + 1
        out_ref[l, pl.ds(pl.multiple_of(k * rows, rows), rows), :] = blocks_ref[t]
        return carry

    lax.fori_loop(0, held, body, 0)
    which = lax.broadcasted_iota(jnp.int32, (NOTE, width), 0)
    for d in range(owners):
        note = jnp.zeros((NOTE, width), jnp.float32)
        for k in range(CAP):
            note = jnp.where(which == k, first[d, k].astype(jnp.float32), note)
        out_ref[d, CAP * rows :, :] = note.astype(out_ref.dtype)


def pick(pairs, blocks, owners):
    held, aux, width, _ = blocks.shape
    rows = aux * width
    return pl.pallas_call(
        pick_kernel,
        out_shape=jax.ShapeDtypeStruct((owners, CAP * rows + NOTE, width), blocks.dtype),
        in_specs=[
            pl.BlockSpec(memory_space=pltpu.SMEM),
            pl.BlockSpec(memory_space=pltpu.VMEM),
        ],
        out_specs=pl.BlockSpec(memory_space=pltpu.VMEM),
        scratch_shapes=[
            pltpu.SMEM((owners,), jnp.int32),
            pltpu.SMEM((owners, CAP), jnp.int32),
        ],
        compiler_params=pltpu.CompilerParams(vmem_limit_bytes=16 * 1024 * 1024),
        cost_estimate=pl.CostEstimate(flops=0, bytes_accessed=4 * blocks.size, transcendentals=0),
        name="pick",
    )(pairs, blocks.reshape(held, rows, width))


def place_kernel(first_ref, *refs):
    slot_refs, out_ref, total = refs[:CAP], refs[CAP], refs[CAP + 1]
    width = total.shape[1]
    total[...] = jnp.zeros_like(total)

    def body(s, carry):
        for k, slots in enumerate(slot_refs):
            m = first_ref[s * CAP + k]

            @pl.when(m >= 0)
            def _():
                rows = pl.ds(pl.multiple_of(m * width, width), width)
                total[rows, :] += slots[s].astype(jnp.float32)

        return carry

    lax.fori_loop(0, slot_refs[0].shape[0], body, 0, unroll=4)
    out_ref[...] = total[...].astype(out_ref.dtype)


def place(first, recv, start, depth, aux, rows):
    senders, _, width = recv.shape

    def slot(k):
        return pl.BlockSpec((senders, width, width), lambda p, first: (0, k * aux + start + p, 0))

    size = senders * CAP * depth * width * width
    return pl.pallas_call(
        place_kernel,
        out_shape=jax.ShapeDtypeStruct((rows, depth * width), recv.dtype),
        grid_spec=pltpu.PrefetchScalarGridSpec(
            num_scalar_prefetch=1,
            grid=(depth,),
            in_specs=[slot(k) for k in range(CAP)],
            out_specs=pl.BlockSpec((rows, width), lambda p, first: (0, p)),
            scratch_shapes=[pltpu.VMEM((rows, width), jnp.float32)],
        ),
        compiler_params=pltpu.CompilerParams(vmem_limit_bytes=8 * 1024 * 1024),
        cost_estimate=pl.CostEstimate(flops=size, bytes_accessed=4 * size, transcendentals=0),
        name="place",
    )(first, *[recv] * CAP)


FROM = (0, -1, 1, 2)


def hop(x, by, first):
    pairs = []
    for device in range(128):
        xl, y, xh, core = device // 16 % 2, device // 4 % 4, device // 2 % 2, device % 2
        if (core == 0) == first:
            to = device + ((y + by) % 4 - y) * 4
        else:
            to_x = (2 * xh + xl + by) % 4
            to = device + (to_x % 2 - xl) * 16 + (to_x // 2 - xh) * 2
        pairs.append((device, to))
    return lax.ppermute(x, AXES, pairs)


def ring(x, first):
    return [x] + [hop(x, by, first) for by in (1, -1, 2)]


def lay_kernel(spots, *refs):
    pieces, out_ref = refs[:-1], refs[-1]
    z, y, core = lax.axis_index("z"), lax.axis_index("y"), lax.axis_index("core")
    x = 2 * lax.axis_index("xh") + lax.axis_index("xl")
    for piece, (dz, start) in zip(pieces, spots, strict=True):
        for i in range(piece.shape[0]):
            late, early = FROM[(start + i) // 4], FROM[(start + i) % 4]
            to_x = (x + 4 + late + (early - late) * core) % 4
            to_y = (y + 4 + early + (late - early) * core) % 4
            out_ref[(z + 4 + dz) % 4, to_x % 2, to_y, to_x // 2] = piece[i]


def lay(spots, pieces):
    _, rows, columns = pieces[0].shape
    out = pl.pallas_call(
        functools.partial(lay_kernel, spots),
        out_shape=jax.ShapeDtypeStruct((*SIZES[:-1], rows, columns), pieces[0].dtype),
        in_specs=[pl.BlockSpec(memory_space=pltpu.VMEM)] * len(pieces),
        out_specs=pl.BlockSpec(memory_space=pltpu.VMEM),
        compiler_params=pltpu.CompilerParams(vmem_limit_bytes=10 * 1024 * 1024),
        cost_estimate=pl.CostEstimate(
            flops=0, bytes_accessed=256 * rows * columns, transcendentals=0
        ),
        name="lay",
    )(*pieces)
    return out.reshape(-1, rows, columns)


def merge_kernel(mine_ref, other_ref, out_ref):
    core = lax.axis_index("core")

    def body(i, carry):
        out_ref[i, core] = mine_ref[i]
        out_ref[i, 1 - core] = other_ref[i]
        return carry

    lax.fori_loop(0, mine_ref.shape[0], body, 0, unroll=2)


def merge(mine, other):
    chips, rows, columns = mine.shape
    out = pl.pallas_call(
        merge_kernel,
        out_shape=jax.ShapeDtypeStruct((chips, 2, rows, columns), mine.dtype),
        in_specs=[pl.BlockSpec(memory_space=pltpu.VMEM)] * 2,
        out_specs=pl.BlockSpec(memory_space=pltpu.VMEM),
        compiler_params=pltpu.CompilerParams(vmem_limit_bytes=20 * 1024 * 1024),
        cost_estimate=pl.CostEstimate(flops=0, bytes_accessed=8 * mine.size, transcendentals=0),
        name="merge",
    )(mine, other)
    return out.reshape(-1, columns)


FORWARDED = ((0, 0), (-1, 0), (1, 0), (2, 0), (2, 8))
DIRECT = ((0, 0), (-1, 0), (1, 0), (2, 0))


def z_forwarded(mine):
    half = mine.shape[0] // 2
    below, above = up(mine), down(mine)
    return [mine, below, above, up(below[:half]), down(above[half:])]


def z_direct(mine):
    return [mine, up(mine), down(mine), up(mine, 2)]


def pair_kernel(x_ref, *refs):
    y_refs, out_ref = refs[:-1], refs[-1]
    blocks, width, _ = x_ref.shape
    aux_x = x_ref.shape[2] // width
    same = lax.broadcasted_iota(jnp.int32, (width, width), 0) == lax.broadcasted_iota(
        jnp.int32, (width, width), 1
    )
    x = jnp.concatenate(
        [
            jnp.concatenate(
                [x_ref[k, :, p * width : (p + 1) * width] for k in range(blocks)], axis=1
            )
            for p in range(aux_x)
        ],
        axis=0,
    )
    done = 0
    for y_ref in y_refs:
        products = lax.dot_general(
            x, y_ref[...], (((1,), (1,)), ((), ())), preferred_element_type=jnp.float32
        )
        aux_y = y_ref.shape[0] // width
        for q in range(aux_y):
            for p in range(aux_x):
                tile = products[p * width : (p + 1) * width, q * width : (q + 1) * width]
                tile = jnp.where(same, tile, 0.0).reshape(width // 8, 8, width)
                out_ref[(done + q) * aux_x + p] = tile.sum(axis=0)
        done += aux_y


def pair_sums(x, ys):
    _, width, _ = x.shape
    aux_x, aux_y = x.shape[2] // width, sum(y.shape[0] for y in ys) // width
    sums = pl.pallas_call(
        pair_kernel,
        out_shape=jax.ShapeDtypeStruct((aux_y * aux_x, 8, width), jnp.float32),
        in_specs=[pl.BlockSpec(memory_space=pltpu.VMEM)] * (1 + len(ys)),
        out_specs=pl.BlockSpec(memory_space=pltpu.VMEM),
        compiler_params=pltpu.CompilerParams(vmem_limit_bytes=16 * 1024 * 1024),
        cost_estimate=pl.CostEstimate(
            flops=2 * x.size * aux_y, bytes_accessed=6 * x.size, transcendentals=0
        ),
        name="pair",
    )(x, *ys)
    return sums.sum(axis=(1, 2)).reshape(aux_y, aux_x).T


def col_sum(x):
    x = x + other_core(x)
    x = x + permute(x, "xh", lambda k: 1 - k)
    x = x + permute(x, "y", lambda k: k ^ 1)
    return x + permute(x, "y", lambda k: 3 - k)


def shards(tensor_blocks, block_list, occ_green, virt_green):
    col_count = lax.axis_size(COL)
    blocks = tensor_blocks[0]
    aux, width = blocks.shape[1], blocks.shape[-1]
    basis_total = occ_green.shape[1]
    shard_rows = occ_green.shape[0]

    picked = pick(block_list[0], blocks, col_count)
    line = ring(jnp.concatenate([occ_green, virt_green.T], axis=0)[None], True)
    plane = ring(jnp.concatenate(line, axis=0), False)
    picked, plane = lax.optimization_barrier((picked, plane))
    plane = jnp.concatenate(plane, axis=0)
    recv = lax.all_to_all(picked, COL, split_axis=0, concat_axis=0, tiled=True)
    notes = CAP * aux * width
    recv_first = recv[:, notes : notes + CAP, 0].astype(jnp.int32).reshape(-1) - 1

    occ_plane, virt_plane = plane[:, :shard_rows], plane[:, shard_rows:]
    occ_pieces = z_forwarded(occ_plane)
    occ_pieces, virt_plane = lax.optimization_barrier((occ_pieces, virt_plane))
    virt_pieces = z_direct(virt_plane)
    occ_mine = lay(FORWARDED, occ_pieces)
    occ = merge(occ_mine, other_core(occ_mine))

    dense, turned, start = [], [], 0
    for depth in CHUNKS:
        dense.append(place(recv_first, recv, start, depth, aux, basis_total))
        half = jnp.dot(occ, dense[-1], preferred_element_type=jnp.float32).astype(jnp.bfloat16)
        cut = half.reshape(col_count, width, -1)
        turned.append(lax.all_to_all(cut, COL, split_axis=0, concat_axis=0, tiled=True))
        recv_first, _ = lax.optimization_barrier((recv_first, half))
        start += depth

    _, virt_pieces = lax.optimization_barrier((half, virt_pieces))
    virt_mine = lay(DIRECT, virt_pieces)
    turned[0], virt_mine = lax.optimization_barrier((turned[0], virt_mine))
    virt_t = merge(virt_mine, other_core(virt_mine))
    virt_half = [
        lax.dot_general(
            d, virt_t, (((0,), (0,)), ((), ())), preferred_element_type=jnp.float32
        ).astype(jnp.bfloat16)
        for d in dense
    ]
    sums = jnp.concatenate([pair_sums(x, virt_half) for x in turned], axis=0)
    return (col_sum(sums) / float(basis_total))[None]


def solution(mesh):
    fine = Mesh(mesh.devices.reshape(SIZES), AXES)
    in_specs = (
        P(ROW, COL, None, None, None),
        P(ROW, COL, None),
        P(ROW + COL, None),
        P(None, ROW + COL),
    )
    return jax.shard_map(
        shards, mesh=fine, in_specs=in_specs, out_specs=P(ROW, None, None), check_vma=False
    )
```

```python
import functools

import jax
import jax.numpy as jnp
from jax import lax
from jax.experimental import pallas as pl
from jax.experimental.pallas import tpu as pltpu
from jax.sharding import Mesh
from jax.sharding import PartitionSpec as P

CAP = 2
CHUNKS = (2, 4)
NOTE = 16
AXES = ("z", "xl", "y", "xh", "core")
SIZES = (4, 2, 4, 2, 2)
COL = ("y", "xh", "core")
ROW = ("z", "xl")


def moved(axis, to):
    where = AXES.index(axis)
    stride = 1
    for size in SIZES[where + 1 :]:
        stride *= size
    total = 1
    for size in SIZES:
        total *= size
    pairs = []
    for device in range(total):
        k = device // stride % SIZES[where]
        pairs.append((device, device + (to(k) - k) * stride))
    return pairs


def permute(x, axis, to):
    return lax.ppermute(x, AXES, moved(axis, to))


def up(x, by=1):
    return permute(x, "z", lambda k: (k + by) % 4)


def down(x):
    return permute(x, "z", lambda k: (k - 1) % 4)


def other_core(x):
    return permute(x, "core", lambda k: 1 - k)


def pick_kernel(pairs_ref, blocks_ref, out_ref, count, first):
    held, rows, width = blocks_ref.shape
    owners = count.shape[0]
    for d in range(owners):
        count[d] = 0
        for k in range(CAP):
            first[d, k] = 0

    def body(t, carry):
        l = pairs_ref[t, 1]
        k = count[l]
        count[l] = k + 1
        first[l, k] = pairs_ref[t, 0] + 1
        out_ref[l, pl.ds(pl.multiple_of(k * rows, rows), rows), :] = blocks_ref[t]
        return carry

    lax.fori_loop(0, held, body, 0)
    which = lax.broadcasted_iota(jnp.int32, (NOTE, width), 0)
    for d in range(owners):
        note = jnp.zeros((NOTE, width), jnp.float32)
        for k in range(CAP):
            note = jnp.where(which == k, first[d, k].astype(jnp.float32), note)
        out_ref[d, CAP * rows :, :] = note.astype(out_ref.dtype)


def pick(pairs, blocks, owners):
    held, aux, width, _ = blocks.shape
    rows = aux * width
    return pl.pallas_call(
        pick_kernel,
        out_shape=jax.ShapeDtypeStruct((owners, CAP * rows + NOTE, width), blocks.dtype),
        in_specs=[
            pl.BlockSpec(memory_space=pltpu.SMEM),
            pl.BlockSpec(memory_space=pltpu.VMEM),
        ],
        out_specs=pl.BlockSpec(memory_space=pltpu.VMEM),
        scratch_shapes=[
            pltpu.SMEM((owners,), jnp.int32),
            pltpu.SMEM((owners, CAP), jnp.int32),
        ],
        compiler_params=pltpu.CompilerParams(vmem_limit_bytes=16 * 1024 * 1024),
        cost_estimate=pl.CostEstimate(flops=0, bytes_accessed=4 * blocks.size, transcendentals=0),
        name="pick",
    )(pairs, blocks.reshape(held, rows, width))


def place_kernel(first_ref, *refs):
    slot_refs, out_ref, total = refs[:CAP], refs[CAP], refs[CAP + 1]
    width = total.shape[1]
    total[...] = jnp.zeros_like(total)

    def body(s, carry):
        for k, slots in enumerate(slot_refs):
            m = first_ref[s * CAP + k]

            @pl.when(m >= 0)
            def _():
                rows = pl.ds(pl.multiple_of(m * width, width), width)
                total[rows, :] += slots[s].astype(jnp.float32)

        return carry

    lax.fori_loop(0, slot_refs[0].shape[0], body, 0, unroll=4)
    out_ref[...] = total[...].astype(out_ref.dtype)


def place(first, recv, start, depth, aux, rows):
    senders, _, width = recv.shape

    def slot(k):
        return pl.BlockSpec((senders, width, width), lambda p, first: (0, k * aux + start + p, 0))

    size = senders * CAP * depth * width * width
    return pl.pallas_call(
        place_kernel,
        out_shape=jax.ShapeDtypeStruct((rows, depth * width), recv.dtype),
        grid_spec=pltpu.PrefetchScalarGridSpec(
            num_scalar_prefetch=1,
            grid=(depth,),
            in_specs=[slot(k) for k in range(CAP)],
            out_specs=pl.BlockSpec((rows, width), lambda p, first: (0, p)),
            scratch_shapes=[pltpu.VMEM((rows, width), jnp.float32)],
        ),
        compiler_params=pltpu.CompilerParams(vmem_limit_bytes=8 * 1024 * 1024),
        cost_estimate=pl.CostEstimate(flops=size, bytes_accessed=4 * size, transcendentals=0),
        name="place",
    )(first, *[recv] * CAP)


FROM = (0, -1, 1, 2)


def hop(x, by, first):
    pairs = []
    for device in range(128):
        xl, y, xh, core = device // 16 % 2, device // 4 % 4, device // 2 % 2, device % 2
        if (core == 0) == first:
            to = device + ((y + by) % 4 - y) * 4
        else:
            to_x = (2 * xh + xl + by) % 4
            to = device + (to_x % 2 - xl) * 16 + (to_x // 2 - xh) * 2
        pairs.append((device, to))
    return lax.ppermute(x, AXES, pairs)


def ring(x, first):
    return [x] + [hop(x, by, first) for by in (1, -1, 2)]


def lay_kernel(spots, *refs):
    pieces, out_ref = refs[:-1], refs[-1]
    z, y, core = lax.axis_index("z"), lax.axis_index("y"), lax.axis_index("core")
    x = 2 * lax.axis_index("xh") + lax.axis_index("xl")
    for piece, (dz, start) in zip(pieces, spots, strict=True):
        for i in range(piece.shape[0]):
            late, early = FROM[(start + i) // 4], FROM[(start + i) % 4]
            to_x = (x + 4 + late + (early - late) * core) % 4
            to_y = (y + 4 + early + (late - early) * core) % 4
            out_ref[(z + 4 + dz) % 4, to_x % 2, to_y, to_x // 2] = piece[i]


def lay(spots, pieces):
    _, rows, columns = pieces[0].shape
    out = pl.pallas_call(
        functools.partial(lay_kernel, spots),
        out_shape=jax.ShapeDtypeStruct((*SIZES[:-1], rows, columns), pieces[0].dtype),
        in_specs=[pl.BlockSpec(memory_space=pltpu.VMEM)] * len(pieces),
        out_specs=pl.BlockSpec(memory_space=pltpu.VMEM),
        compiler_params=pltpu.CompilerParams(vmem_limit_bytes=10 * 1024 * 1024),
        cost_estimate=pl.CostEstimate(
            flops=0, bytes_accessed=256 * rows * columns, transcendentals=0
        ),
        name="lay",
    )(*pieces)
    return out.reshape(-1, rows, columns)


def merge_kernel(mine_ref, other_ref, out_ref):
    core = lax.axis_index("core")

    def body(i, carry):
        out_ref[i, core] = mine_ref[i]
        out_ref[i, 1 - core] = other_ref[i]
        return carry

    lax.fori_loop(0, mine_ref.shape[0], body, 0, unroll=2)


def merge(mine, other):
    chips, rows, columns = mine.shape
    out = pl.pallas_call(
        merge_kernel,
        out_shape=jax.ShapeDtypeStruct((chips, 2, rows, columns), mine.dtype),
        in_specs=[pl.BlockSpec(memory_space=pltpu.VMEM)] * 2,
        out_specs=pl.BlockSpec(memory_space=pltpu.VMEM),
        compiler_params=pltpu.CompilerParams(vmem_limit_bytes=20 * 1024 * 1024),
        cost_estimate=pl.CostEstimate(flops=0, bytes_accessed=8 * mine.size, transcendentals=0),
        name="merge",
    )(mine, other)
    return out.reshape(-1, columns)


FORWARDED = ((0, 0), (-1, 0), (1, 0), (2, 0), (2, 8))
DIRECT = ((0, 0), (-1, 0), (1, 0), (2, 0))


def z_forwarded(mine):
    half = mine.shape[0] // 2
    below, above = up(mine), down(mine)
    return [mine, below, above, up(below[:half]), down(above[half:])]


def z_direct(mine):
    return [mine, up(mine), down(mine), up(mine, 2)]


def pair_kernel(x_ref, *refs):
    y_refs, out_ref = refs[:-1], refs[-1]
    blocks, width, _ = x_ref.shape
    aux_x = x_ref.shape[2] // width
    same = lax.broadcasted_iota(jnp.int32, (width, width), 0) == lax.broadcasted_iota(
        jnp.int32, (width, width), 1
    )
    x = jnp.concatenate(
        [
            jnp.concatenate(
                [x_ref[k, :, p * width : (p + 1) * width] for k in range(blocks)], axis=1
            )
            for p in range(aux_x)
        ],
        axis=0,
    )
    done = 0
    for y_ref in y_refs:
        products = lax.dot_general(
            x, y_ref[...], (((1,), (1,)), ((), ())), preferred_element_type=jnp.float32
        )
        aux_y = y_ref.shape[0] // width
        for q in range(aux_y):
            for p in range(aux_x):
                tile = products[p * width : (p + 1) * width, q * width : (q + 1) * width]
                tile = jnp.where(same, tile, 0.0).reshape(width // 8, 8, width)
                out_ref[(done + q) * aux_x + p] = tile.sum(axis=0)
        done += aux_y


def pair_sums(x, ys):
    _, width, _ = x.shape
    aux_x, aux_y = x.shape[2] // width, sum(y.shape[0] for y in ys) // width
    sums = pl.pallas_call(
        pair_kernel,
        out_shape=jax.ShapeDtypeStruct((aux_y * aux_x, 8, width), jnp.float32),
        in_specs=[pl.BlockSpec(memory_space=pltpu.VMEM)] * (1 + len(ys)),
        out_specs=pl.BlockSpec(memory_space=pltpu.VMEM),
        compiler_params=pltpu.CompilerParams(vmem_limit_bytes=16 * 1024 * 1024),
        cost_estimate=pl.CostEstimate(
            flops=2 * x.size * aux_y, bytes_accessed=6 * x.size, transcendentals=0
        ),
        name="pair",
    )(x, *ys)
    return sums.sum(axis=(1, 2)).reshape(aux_y, aux_x).T


def col_sum(x):
    x = x + other_core(x)
    x = x + permute(x, "xh", lambda k: 1 - k)
    x = x + permute(x, "y", lambda k: k ^ 1)
    return x + permute(x, "y", lambda k: 3 - k)


def shards(tensor_blocks, block_list, occ_green, virt_green):
    col_count = lax.axis_size(COL)
    blocks = tensor_blocks[0]
    aux, width = blocks.shape[1], blocks.shape[-1]
    basis_total = occ_green.shape[1]
    shard_rows = occ_green.shape[0]

    picked = pick(block_list[0], blocks, col_count)
    line = ring(jnp.concatenate([occ_green, virt_green.T], axis=0)[None], True)
    line = jnp.concatenate(line, axis=0)
    picked, line = lax.optimization_barrier((picked, line))
    plane = ring(line, False)
    plane = jnp.concatenate(plane, axis=0)
    recv = lax.all_to_all(picked, COL, split_axis=0, concat_axis=0, tiled=True)
    notes = CAP * aux * width
    recv_first = recv[:, notes : notes + CAP, 0].astype(jnp.int32).reshape(-1) - 1

    occ_plane, virt_plane = plane[:, :shard_rows], plane[:, shard_rows:]
    occ_pieces = z_forwarded(occ_plane)
    occ_pieces, virt_plane = lax.optimization_barrier((occ_pieces, virt_plane))
    virt_pieces = z_direct(virt_plane)
    occ_mine = lay(FORWARDED, occ_pieces)
    occ = merge(occ_mine, other_core(occ_mine))

    dense, turned, start = [], [], 0
    for depth in CHUNKS:
        dense.append(place(recv_first, recv, start, depth, aux, basis_total))
        half = jnp.dot(occ, dense[-1], preferred_element_type=jnp.float32).astype(jnp.bfloat16)
        cut = half.reshape(col_count, width, -1)
        turned.append(lax.all_to_all(cut, COL, split_axis=0, concat_axis=0, tiled=True))
        recv_first, _ = lax.optimization_barrier((recv_first, half))
        start += depth

    turned[0], _, virt_pieces = lax.optimization_barrier((turned[0], half, virt_pieces))
    virt_mine = lay(DIRECT, virt_pieces)
    virt_t = merge(virt_mine, other_core(virt_mine))
    virt_half = [
        lax.dot_general(
            d, virt_t, (((0,), (0,)), ((), ())), preferred_element_type=jnp.float32
        ).astype(jnp.bfloat16)
        for d in dense
    ]
    sums = jnp.concatenate([pair_sums(x, virt_half) for x in turned], axis=0)
    return (col_sum(sums) / float(basis_total))[None]


def solution(mesh):
    fine = Mesh(mesh.devices.reshape(SIZES), AXES)
    in_specs = (
        P(ROW, COL, None, None, None),
        P(ROW, COL, None),
        P(ROW + COL, None),
        P(None, ROW + COL),
    )
    return jax.shard_map(
        shards, mesh=fine, in_specs=in_specs, out_specs=P(ROW, None, None), check_vma=False
    )
```

```python
import functools

import jax
import jax.numpy as jnp
from jax import lax
from jax.experimental import pallas as pl
from jax.experimental.pallas import tpu as pltpu
from jax.sharding import Mesh
from jax.sharding import PartitionSpec as P

CAP = 2
CHUNKS = (2, 4)
NOTE = 16
AXES = ("z", "xl", "y", "xh", "core")
SIZES = (4, 2, 4, 2, 2)
COL = ("y", "xh", "core")
ROW = ("z", "xl")


def moved(axis, to):
    where = AXES.index(axis)
    stride = 1
    for size in SIZES[where + 1 :]:
        stride *= size
    total = 1
    for size in SIZES:
        total *= size
    pairs = []
    for device in range(total):
        k = device // stride % SIZES[where]
        pairs.append((device, device + (to(k) - k) * stride))
    return pairs


def permute(x, axis, to):
    return lax.ppermute(x, AXES, moved(axis, to))


def up(x, by=1):
    return permute(x, "z", lambda k: (k + by) % 4)


def down(x):
    return permute(x, "z", lambda k: (k - 1) % 4)


def other_core(x):
    return permute(x, "core", lambda k: 1 - k)


def pick_kernel(pairs_ref, blocks_ref, out_ref, count, first):
    held, rows, width = blocks_ref.shape
    owners = count.shape[0]
    for d in range(owners):
        count[d] = 0
        for k in range(CAP):
            first[d, k] = 0

    def body(t, carry):
        l = pairs_ref[t, 1]
        k = count[l]
        count[l] = k + 1
        first[l, k] = pairs_ref[t, 0] + 1
        out_ref[l, pl.ds(pl.multiple_of(k * rows, rows), rows), :] = blocks_ref[t]
        return carry

    lax.fori_loop(0, held, body, 0)
    which = lax.broadcasted_iota(jnp.int32, (NOTE, width), 0)
    for d in range(owners):
        note = jnp.zeros((NOTE, width), jnp.float32)
        for k in range(CAP):
            note = jnp.where(which == k, first[d, k].astype(jnp.float32), note)
        out_ref[d, CAP * rows :, :] = note.astype(out_ref.dtype)


def pick(pairs, blocks, owners):
    held, aux, width, _ = blocks.shape
    rows = aux * width
    return pl.pallas_call(
        pick_kernel,
        out_shape=jax.ShapeDtypeStruct((owners, CAP * rows + NOTE, width), blocks.dtype),
        in_specs=[
            pl.BlockSpec(memory_space=pltpu.SMEM),
            pl.BlockSpec(memory_space=pltpu.VMEM),
        ],
        out_specs=pl.BlockSpec(memory_space=pltpu.VMEM),
        scratch_shapes=[
            pltpu.SMEM((owners,), jnp.int32),
            pltpu.SMEM((owners, CAP), jnp.int32),
        ],
        compiler_params=pltpu.CompilerParams(vmem_limit_bytes=16 * 1024 * 1024),
        cost_estimate=pl.CostEstimate(flops=0, bytes_accessed=4 * blocks.size, transcendentals=0),
        name="pick",
    )(pairs, blocks.reshape(held, rows, width))


def place_kernel(first_ref, *refs):
    slot_refs, out_ref, total = refs[:CAP], refs[CAP], refs[CAP + 1]
    width = total.shape[1]
    total[...] = jnp.zeros_like(total)

    def body(s, carry):
        for k, slots in enumerate(slot_refs):
            m = first_ref[s * CAP + k]

            @pl.when(m >= 0)
            def _():
                rows = pl.ds(pl.multiple_of(m * width, width), width)
                total[rows, :] += slots[s].astype(jnp.float32)

        return carry

    lax.fori_loop(0, slot_refs[0].shape[0], body, 0, unroll=4)
    out_ref[...] = total[...].astype(out_ref.dtype)


def place(first, recv, start, depth, aux, rows):
    senders, _, width = recv.shape

    def slot(k):
        return pl.BlockSpec((senders, width, width), lambda p, first: (0, k * aux + start + p, 0))

    size = senders * CAP * depth * width * width
    return pl.pallas_call(
        place_kernel,
        out_shape=jax.ShapeDtypeStruct((rows, depth * width), recv.dtype),
        grid_spec=pltpu.PrefetchScalarGridSpec(
            num_scalar_prefetch=1,
            grid=(depth,),
            in_specs=[slot(k) for k in range(CAP)],
            out_specs=pl.BlockSpec((rows, width), lambda p, first: (0, p)),
            scratch_shapes=[pltpu.VMEM((rows, width), jnp.float32)],
        ),
        compiler_params=pltpu.CompilerParams(vmem_limit_bytes=8 * 1024 * 1024),
        cost_estimate=pl.CostEstimate(flops=size, bytes_accessed=4 * size, transcendentals=0),
        name="place",
    )(first, *[recv] * CAP)


FROM = (0, -1, 1, 2)


def hop(x, by, first):
    pairs = []
    for device in range(128):
        xl, y, xh, core = device // 16 % 2, device // 4 % 4, device // 2 % 2, device % 2
        if (core == 0) == first:
            to = device + ((y + by) % 4 - y) * 4
        else:
            to_x = (2 * xh + xl + by) % 4
            to = device + (to_x % 2 - xl) * 16 + (to_x // 2 - xh) * 2
        pairs.append((device, to))
    return lax.ppermute(x, AXES, pairs)


def ring(x, first):
    return [x] + [hop(x, by, first) for by in (1, -1, 2)]


def lay_kernel(spots, *refs):
    pieces, out_ref = refs[:-1], refs[-1]
    z, y, core = lax.axis_index("z"), lax.axis_index("y"), lax.axis_index("core")
    x = 2 * lax.axis_index("xh") + lax.axis_index("xl")
    for piece, (dz, start) in zip(pieces, spots, strict=True):
        for i in range(piece.shape[0]):
            late, early = FROM[(start + i) // 4], FROM[(start + i) % 4]
            to_x = (x + 4 + late + (early - late) * core) % 4
            to_y = (y + 4 + early + (late - early) * core) % 4
            out_ref[(z + 4 + dz) % 4, to_x % 2, to_y, to_x // 2] = piece[i]


def lay(spots, pieces):
    _, rows, columns = pieces[0].shape
    out = pl.pallas_call(
        functools.partial(lay_kernel, spots),
        out_shape=jax.ShapeDtypeStruct((*SIZES[:-1], rows, columns), pieces[0].dtype),
        in_specs=[pl.BlockSpec(memory_space=pltpu.VMEM)] * len(pieces),
        out_specs=pl.BlockSpec(memory_space=pltpu.VMEM),
        compiler_params=pltpu.CompilerParams(vmem_limit_bytes=10 * 1024 * 1024),
        cost_estimate=pl.CostEstimate(
            flops=0, bytes_accessed=256 * rows * columns, transcendentals=0
        ),
        name="lay",
    )(*pieces)
    return out.reshape(-1, rows, columns)


def merge_kernel(mine_ref, other_ref, out_ref):
    core = lax.axis_index("core")

    def body(i, carry):
        out_ref[i, core] = mine_ref[i]
        out_ref[i, 1 - core] = other_ref[i]
        return carry

    lax.fori_loop(0, mine_ref.shape[0], body, 0, unroll=2)


def merge(mine, other):
    chips, rows, columns = mine.shape
    out = pl.pallas_call(
        merge_kernel,
        out_shape=jax.ShapeDtypeStruct((chips, 2, rows, columns), mine.dtype),
        in_specs=[pl.BlockSpec(memory_space=pltpu.VMEM)] * 2,
        out_specs=pl.BlockSpec(memory_space=pltpu.VMEM),
        compiler_params=pltpu.CompilerParams(vmem_limit_bytes=20 * 1024 * 1024),
        cost_estimate=pl.CostEstimate(flops=0, bytes_accessed=8 * mine.size, transcendentals=0),
        name="merge",
    )(mine, other)
    return out.reshape(-1, columns)


FORWARDED = ((0, 0), (-1, 0), (1, 0), (2, 0), (2, 8))
DIRECT = ((0, 0), (-1, 0), (1, 0), (2, 0))


def z_forwarded(mine):
    half = mine.shape[0] // 2
    below, above = up(mine), down(mine)
    return [mine, below, above, up(below[:half]), down(above[half:])]


def z_direct(mine):
    return [mine, up(mine), down(mine), up(mine, 2)]


def pair_kernel(x_ref, *refs):
    y_refs, out_ref = refs[:-1], refs[-1]
    blocks, width, _ = x_ref.shape
    aux_x = x_ref.shape[2] // width
    same = lax.broadcasted_iota(jnp.int32, (width, width), 0) == lax.broadcasted_iota(
        jnp.int32, (width, width), 1
    )
    x = jnp.concatenate(
        [
            jnp.concatenate(
                [x_ref[k, :, p * width : (p + 1) * width] for k in range(blocks)], axis=1
            )
            for p in range(aux_x)
        ],
        axis=0,
    )
    done = 0
    for y_ref in y_refs:
        products = lax.dot_general(
            x, y_ref[...], (((1,), (1,)), ((), ())), preferred_element_type=jnp.float32
        )
        aux_y = y_ref.shape[0] // width
        for q in range(aux_y):
            for p in range(aux_x):
                tile = products[p * width : (p + 1) * width, q * width : (q + 1) * width]
                tile = jnp.where(same, tile, 0.0).reshape(width // 8, 8, width)
                out_ref[(done + q) * aux_x + p] = tile.sum(axis=0)
        done += aux_y


def pair_sums(x, ys):
    _, width, _ = x.shape
    aux_x, aux_y = x.shape[2] // width, sum(y.shape[0] for y in ys) // width
    sums = pl.pallas_call(
        pair_kernel,
        out_shape=jax.ShapeDtypeStruct((aux_y * aux_x, 8, width), jnp.float32),
        in_specs=[pl.BlockSpec(memory_space=pltpu.VMEM)] * (1 + len(ys)),
        out_specs=pl.BlockSpec(memory_space=pltpu.VMEM),
        compiler_params=pltpu.CompilerParams(vmem_limit_bytes=16 * 1024 * 1024),
        cost_estimate=pl.CostEstimate(
            flops=2 * x.size * aux_y, bytes_accessed=6 * x.size, transcendentals=0
        ),
        name="pair",
    )(x, *ys)
    return sums.sum(axis=(1, 2)).reshape(aux_y, aux_x).T


def col_sum(x):
    x = x + other_core(x)
    x = x + permute(x, "xh", lambda k: 1 - k)
    x = x + permute(x, "y", lambda k: k ^ 1)
    return x + permute(x, "y", lambda k: 3 - k)


def shards(tensor_blocks, block_list, occ_green, virt_green):
    col_count = lax.axis_size(COL)
    blocks = tensor_blocks[0]
    aux, width = blocks.shape[1], blocks.shape[-1]
    basis_total = occ_green.shape[1]
    shard_rows = occ_green.shape[0]

    picked = pick(block_list[0], blocks, col_count)
    line = ring(jnp.concatenate([occ_green, virt_green.T], axis=0)[None], True)
    plane = ring(jnp.concatenate(line, axis=0), False)
    picked, plane = lax.optimization_barrier((picked, plane))
    plane = jnp.concatenate(plane, axis=0)
    recv = lax.all_to_all(picked, COL, split_axis=0, concat_axis=0, tiled=True)
    notes = CAP * aux * width
    recv_first = recv[:, notes : notes + CAP, 0].astype(jnp.int32).reshape(-1) - 1

    occ_plane, virt_plane = plane[:, :shard_rows], plane[:, shard_rows:]
    occ_pieces = z_forwarded(occ_plane)
    occ_pieces, virt_plane = lax.optimization_barrier((occ_pieces, virt_plane))
    virt_pieces = z_direct(virt_plane)
    occ_mine = lay(FORWARDED, occ_pieces)
    occ = merge(occ_mine, other_core(occ_mine))

    dense, turned, start = [], [], 0
    for depth in CHUNKS:
        dense.append(place(recv_first, recv, start, depth, aux, basis_total))
        half = jnp.dot(occ, dense[-1], preferred_element_type=jnp.float32).astype(jnp.bfloat16)
        cut = half.reshape(col_count, width, -1)
        turned.append(lax.all_to_all(cut, COL, split_axis=0, concat_axis=0, tiled=True))
        recv_first, _ = lax.optimization_barrier((recv_first, half))
        start += depth

    turned[0], _, virt_pieces = lax.optimization_barrier((turned[0], half, virt_pieces))
    virt_mine = lay(DIRECT, virt_pieces)
    virt_t = merge(virt_mine, other_core(virt_mine))
    virt_half = [
        lax.dot_general(
            d, virt_t, (((0,), (0,)), ((), ())), preferred_element_type=jnp.float32
        ).astype(jnp.bfloat16)
        for d in dense
    ]
    sums = jnp.concatenate([pair_sums(x, virt_half) for x in turned], axis=0)
    return (col_sum(sums) / float(basis_total))[None]


def solution(mesh):
    fine = Mesh(mesh.devices.reshape(SIZES), AXES)
    in_specs = (
        P(ROW, COL, None, None, None),
        P(ROW, COL, None),
        P(ROW + COL, None),
        P(None, ROW + COL),
    )
    return jax.shard_map(
        shards, mesh=fine, in_specs=in_specs, out_specs=P(ROW, None, None), check_vma=False
    )
```

```python
import functools

import jax
import jax.numpy as jnp
from jax import lax
from jax.experimental import pallas as pl
from jax.experimental.pallas import tpu as pltpu
from jax.sharding import Mesh
from jax.sharding import PartitionSpec as P

CAP = 2
CHUNKS = (3, 3)
NOTE = 16
AXES = ("z", "xl", "y", "xh", "core")
SIZES = (4, 2, 4, 2, 2)
COL = ("y", "xh", "core")
ROW = ("z", "xl")


def moved(axis, to):
    where = AXES.index(axis)
    stride = 1
    for size in SIZES[where + 1 :]:
        stride *= size
    total = 1
    for size in SIZES:
        total *= size
    pairs = []
    for device in range(total):
        k = device // stride % SIZES[where]
        pairs.append((device, device + (to(k) - k) * stride))
    return pairs


def permute(x, axis, to):
    return lax.ppermute(x, AXES, moved(axis, to))


def up(x, by=1):
    return permute(x, "z", lambda k: (k + by) % 4)


def down(x):
    return permute(x, "z", lambda k: (k - 1) % 4)


def other_core(x):
    return permute(x, "core", lambda k: 1 - k)


def pick_kernel(pairs_ref, blocks_ref, out_ref, count, first):
    held, rows, width = blocks_ref.shape
    owners = count.shape[0]
    for d in range(owners):
        count[d] = 0
        for k in range(CAP):
            first[d, k] = 0

    def body(t, carry):
        l = pairs_ref[t, 1]
        k = count[l]
        count[l] = k + 1
        first[l, k] = pairs_ref[t, 0] + 1
        out_ref[l, pl.ds(pl.multiple_of(k * rows, rows), rows), :] = blocks_ref[t]
        return carry

    lax.fori_loop(0, held, body, 0)
    which = lax.broadcasted_iota(jnp.int32, (NOTE, width), 0)
    for d in range(owners):
        note = jnp.zeros((NOTE, width), jnp.float32)
        for k in range(CAP):
            note = jnp.where(which == k, first[d, k].astype(jnp.float32), note)
        out_ref[d, CAP * rows :, :] = note.astype(out_ref.dtype)


def pick(pairs, blocks, owners):
    held, aux, width, _ = blocks.shape
    rows = aux * width
    return pl.pallas_call(
        pick_kernel,
        out_shape=jax.ShapeDtypeStruct((owners, CAP * rows + NOTE, width), blocks.dtype),
        in_specs=[
            pl.BlockSpec(memory_space=pltpu.SMEM),
            pl.BlockSpec(memory_space=pltpu.VMEM),
        ],
        out_specs=pl.BlockSpec(memory_space=pltpu.VMEM),
        scratch_shapes=[
            pltpu.SMEM((owners,), jnp.int32),
            pltpu.SMEM((owners, CAP), jnp.int32),
        ],
        compiler_params=pltpu.CompilerParams(vmem_limit_bytes=16 * 1024 * 1024),
        cost_estimate=pl.CostEstimate(flops=0, bytes_accessed=4 * blocks.size, transcendentals=0),
        name="pick",
    )(pairs, blocks.reshape(held, rows, width))


def place_kernel(first_ref, *refs):
    slot_refs, out_ref, total = refs[:CAP], refs[CAP], refs[CAP + 1]
    width = total.shape[1]
    total[...] = jnp.zeros_like(total)

    def body(s, carry):
        for k, slots in enumerate(slot_refs):
            m = first_ref[s * CAP + k]

            @pl.when(m >= 0)
            def _():
                rows = pl.ds(pl.multiple_of(m * width, width), width)
                total[rows, :] += slots[s].astype(jnp.float32)

        return carry

    lax.fori_loop(0, slot_refs[0].shape[0], body, 0, unroll=4)
    out_ref[...] = total[...].astype(out_ref.dtype)


def place(first, recv, start, depth, aux, rows):
    senders, _, width = recv.shape

    def slot(k):
        return pl.BlockSpec((senders, width, width), lambda p, first: (0, k * aux + start + p, 0))

    size = senders * CAP * depth * width * width
    return pl.pallas_call(
        place_kernel,
        out_shape=jax.ShapeDtypeStruct((rows, depth * width), recv.dtype),
        grid_spec=pltpu.PrefetchScalarGridSpec(
            num_scalar_prefetch=1,
            grid=(depth,),
            in_specs=[slot(k) for k in range(CAP)],
            out_specs=pl.BlockSpec((rows, width), lambda p, first: (0, p)),
            scratch_shapes=[pltpu.VMEM((rows, width), jnp.float32)],
        ),
        compiler_params=pltpu.CompilerParams(vmem_limit_bytes=8 * 1024 * 1024),
        cost_estimate=pl.CostEstimate(flops=size, bytes_accessed=4 * size, transcendentals=0),
        name="place",
    )(first, *[recv] * CAP)


FROM = (0, -1, 1, 2)


def hop(x, by, first):
    pairs = []
    for device in range(128):
        xl, y, xh, core = device // 16 % 2, device // 4 % 4, device // 2 % 2, device % 2
        if (core == 0) == first:
            to = device + ((y + by) % 4 - y) * 4
        else:
            to_x = (2 * xh + xl + by) % 4
            to = device + (to_x % 2 - xl) * 16 + (to_x // 2 - xh) * 2
        pairs.append((device, to))
    return lax.ppermute(x, AXES, pairs)


def ring(x, first):
    return [x] + [hop(x, by, first) for by in (1, -1, 2)]


def lay_kernel(spots, *refs):
    pieces, out_ref = refs[:-1], refs[-1]
    z, y, core = lax.axis_index("z"), lax.axis_index("y"), lax.axis_index("core")
    x = 2 * lax.axis_index("xh") + lax.axis_index("xl")
    for piece, (side, dz, start) in zip(pieces, spots, strict=True):
        source = (core + side) % 2
        for i in range(piece.shape[0]):
            late, early = FROM[(start + i) // 4], FROM[(start + i) % 4]
            to_x = (x + 4 + late + (early - late) * source) % 4
            to_y = (y + 4 + early + (late - early) * source) % 4
            out_ref[(z + 4 + dz) % 4, to_x % 2, to_y, to_x // 2, source] = piece[i]


def lay(spots, pieces):
    _, rows, columns = pieces[0].shape
    out = pl.pallas_call(
        functools.partial(lay_kernel, spots),
        out_shape=jax.ShapeDtypeStruct((*SIZES, rows, columns), pieces[0].dtype),
        in_specs=[pl.BlockSpec(memory_space=pltpu.VMEM)] * len(pieces),
        out_specs=pl.BlockSpec(memory_space=pltpu.VMEM),
        compiler_params=pltpu.CompilerParams(vmem_limit_bytes=20 * 1024 * 1024),
        cost_estimate=pl.CostEstimate(
            flops=0, bytes_accessed=512 * rows * columns, transcendentals=0
        ),
        name="lay",
    )(*pieces)
    return out.reshape(-1, columns)


FORWARDED = ((0, 0), (-1, 0), (1, 0), (2, 0), (2, 8))
DIRECT = ((0, 0), (-1, 0), (1, 0), (2, 0))


def z_forwarded(mine):
    half = mine.shape[0] // 2
    below, above = up(mine), down(mine)
    return [mine, below, above, up(below[:half]), down(above[half:])]


def z_direct(mine):
    return [mine, up(mine), down(mine), up(mine, 2)]


def assemble(spots, pieces, copies):
    spots = [(side, *spot) for side in range(2) for spot in spots]
    return lay(spots, pieces + copies)


def pair_kernel(x_ref, *refs):
    count = (len(refs) - 4) // 2
    y_refs, out_ref, x_here = refs[:count], refs[count], refs[count + 1]
    y_here, x_sem, y_sems = refs[count + 2 : -2], refs[-2], refs[-1]
    blocks, width, columns = x_ref.shape
    aux_x = columns // width
    for k in range(blocks):
        for p in range(aux_x):
            pltpu.make_async_copy(
                x_ref.at[k, :, pl.ds(p * width, width)],
                x_here.at[pl.ds(p * width, width), pl.ds(k * width, width)],
                x_sem,
            ).start()
    loads = [
        pltpu.make_async_copy(y_ref, here, y_sems.at[i])
        for i, (y_ref, here) in enumerate(zip(y_refs, y_here, strict=True))
    ]
    for load in loads:
        load.start()
    same = lax.broadcasted_iota(jnp.int32, (width, width), 0) == lax.broadcasted_iota(
        jnp.int32, (width, width), 1
    )
    pltpu.make_async_copy(x_here, x_here, x_sem).wait()
    done = 0
    for load, here in zip(loads, y_here, strict=True):
        load.wait()
        products = lax.dot_general(
            x_here[...], here[...], (((1,), (1,)), ((), ())), preferred_element_type=jnp.float32
        )
        aux_y = here.shape[0] // width
        for q in range(aux_y):
            for p in range(aux_x):
                tile = products[p * width : (p + 1) * width, q * width : (q + 1) * width]
                out_ref[(done + q) * aux_x + p, :] = jnp.where(same, tile, 0.0).sum(axis=0)
        done += aux_y


def pair_sums(x, ys):
    blocks, width, columns = x.shape
    aux_x, aux_y = columns // width, sum(y.shape[0] for y in ys) // width
    sums = pl.pallas_call(
        pair_kernel,
        out_shape=jax.ShapeDtypeStruct((aux_y * aux_x, width), jnp.float32),
        in_specs=[pl.BlockSpec(memory_space=pl.ANY)] * (1 + len(ys)),
        out_specs=pl.BlockSpec(memory_space=pltpu.VMEM),
        scratch_shapes=[pltpu.VMEM((columns, blocks * width), x.dtype)]
        + [pltpu.VMEM(y.shape, y.dtype) for y in ys]
        + [pltpu.SemaphoreType.DMA, pltpu.SemaphoreType.DMA((len(ys),))],
        compiler_params=pltpu.CompilerParams(vmem_limit_bytes=60 * 1024 * 1024),
        cost_estimate=pl.CostEstimate(
            flops=2 * x.size * aux_y, bytes_accessed=6 * x.size, transcendentals=0
        ),
        name="pair",
    )(x, *ys)
    return sums.sum(axis=1).reshape(aux_y, aux_x).T


def col_sum(x):
    x = x + other_core(x)
    x = x + permute(x, "xh", lambda k: 1 - k)
    x = x + permute(x, "y", lambda k: k ^ 1)
    return x + permute(x, "y", lambda k: 3 - k)


def shards(tensor_blocks, block_list, occ_green, virt_green):
    col_count = lax.axis_size(COL)
    blocks = tensor_blocks[0]
    aux, width = blocks.shape[1], blocks.shape[-1]
    basis_total = occ_green.shape[1]
    shard_rows = occ_green.shape[0]

    picked = pick(block_list[0], blocks, col_count)
    line = ring(jnp.concatenate([occ_green, virt_green.T], axis=0)[None], True)
    plane = ring(jnp.concatenate(line, axis=0), False)
    picked, plane = lax.optimization_barrier((picked, plane))
    plane = jnp.concatenate(plane, axis=0)
    recv = lax.all_to_all(picked, COL, split_axis=0, concat_axis=0, tiled=True)
    notes = CAP * aux * width
    recv_first = recv[:, notes : notes + CAP, 0].astype(jnp.int32).reshape(-1) - 1

    occ_plane, virt_plane = plane[:, :shard_rows], plane[:, shard_rows:]
    occ_pieces = z_forwarded(occ_plane)
    occ_pieces, virt_plane = lax.optimization_barrier((occ_pieces, virt_plane))
    virt_pieces = z_direct(virt_plane)
    occ = assemble(FORWARDED, occ_pieces, [other_core(p) for p in occ_pieces])

    dense, turned, start = [], [], 0
    for depth in CHUNKS:
        dense.append(place(recv_first, recv, start, depth, aux, basis_total))
        half = jnp.dot(occ, dense[-1], preferred_element_type=jnp.float32).astype(jnp.bfloat16)
        cut = half.reshape(col_count, width, -1)
        turned.append(lax.all_to_all(cut, COL, split_axis=0, concat_axis=0, tiled=True))
        start += depth

    _, virt_pieces = lax.optimization_barrier((half, virt_pieces))
    virt_copies = [other_core(p) for p in virt_pieces]
    turned[0], virt_copies = lax.optimization_barrier((turned[0], virt_copies))
    virt_t = assemble(DIRECT, virt_pieces, virt_copies)
    virt_half = [
        lax.dot_general(
            d, virt_t, (((0,), (0,)), ((), ())), preferred_element_type=jnp.float32
        ).astype(jnp.bfloat16)
        for d in dense
    ]
    sums = jnp.concatenate([pair_sums(x, virt_half) for x in turned], axis=0)
    return (col_sum(sums) / float(basis_total))[None]


def solution(mesh):
    fine = Mesh(mesh.devices.reshape(SIZES), AXES)
    in_specs = (
        P(ROW, COL, None, None, None),
        P(ROW, COL, None),
        P(ROW + COL, None),
        P(None, ROW + COL),
    )
    return jax.shard_map(
        shards, mesh=fine, in_specs=in_specs, out_specs=P(ROW, None, None), check_vma=False
    )
```

```python
import functools

import jax
import jax.numpy as jnp
from jax import lax
from jax.experimental import pallas as pl
from jax.experimental.pallas import tpu as pltpu
from jax.sharding import Mesh
from jax.sharding import PartitionSpec as P

CAP = 2
CHUNKS = (3, 3)
NOTE = 16
AXES = ("z", "xl", "y", "xh", "core")
SIZES = (4, 2, 4, 2, 2)
COL = ("y", "xh", "core")
ROW = ("z", "xl")


def moved(axis, to):
    where = AXES.index(axis)
    stride = 1
    for size in SIZES[where + 1 :]:
        stride *= size
    total = 1
    for size in SIZES:
        total *= size
    pairs = []
    for device in range(total):
        k = device // stride % SIZES[where]
        pairs.append((device, device + (to(k) - k) * stride))
    return pairs


def permute(x, axis, to):
    return lax.ppermute(x, AXES, moved(axis, to))


def up(x, by=1):
    return permute(x, "z", lambda k: (k + by) % 4)


def down(x):
    return permute(x, "z", lambda k: (k - 1) % 4)


def other_core(x):
    return permute(x, "core", lambda k: 1 - k)


def pick_kernel(pairs_ref, blocks_ref, out_ref, count, first):
    held, rows, width = blocks_ref.shape
    owners = count.shape[0]
    for d in range(owners):
        count[d] = 0
        for k in range(CAP):
            first[d, k] = 0

    def body(t, carry):
        l = pairs_ref[t, 1]
        k = count[l]
        count[l] = k + 1
        first[l, k] = pairs_ref[t, 0] + 1
        out_ref[l, pl.ds(pl.multiple_of(k * rows, rows), rows), :] = blocks_ref[t]
        return carry

    lax.fori_loop(0, held, body, 0)
    which = lax.broadcasted_iota(jnp.int32, (NOTE, width), 0)
    for d in range(owners):
        note = jnp.zeros((NOTE, width), jnp.float32)
        for k in range(CAP):
            note = jnp.where(which == k, first[d, k].astype(jnp.float32), note)
        out_ref[d, CAP * rows :, :] = note.astype(out_ref.dtype)


def pick(pairs, blocks, owners):
    held, aux, width, _ = blocks.shape
    rows = aux * width
    return pl.pallas_call(
        pick_kernel,
        out_shape=jax.ShapeDtypeStruct((owners, CAP * rows + NOTE, width), blocks.dtype),
        in_specs=[
            pl.BlockSpec(memory_space=pltpu.SMEM),
            pl.BlockSpec(memory_space=pltpu.VMEM),
        ],
        out_specs=pl.BlockSpec(memory_space=pltpu.VMEM),
        scratch_shapes=[
            pltpu.SMEM((owners,), jnp.int32),
            pltpu.SMEM((owners, CAP), jnp.int32),
        ],
        compiler_params=pltpu.CompilerParams(vmem_limit_bytes=16 * 1024 * 1024),
        cost_estimate=pl.CostEstimate(flops=0, bytes_accessed=4 * blocks.size, transcendentals=0),
        name="pick",
    )(pairs, blocks.reshape(held, rows, width))


def place_kernel(first_ref, *refs):
    slot_refs, out_ref, total = refs[:CAP], refs[CAP], refs[CAP + 1]
    width = total.shape[1]
    total[...] = jnp.zeros_like(total)

    def body(s, carry):
        for k, slots in enumerate(slot_refs):
            m = first_ref[s * CAP + k]

            @pl.when(m >= 0)
            def _():
                rows = pl.ds(pl.multiple_of(m * width, width), width)
                total[rows, :] += slots[s].astype(jnp.float32)

        return carry

    lax.fori_loop(0, slot_refs[0].shape[0], body, 0, unroll=True)
    out_ref[...] = total[...].astype(out_ref.dtype)


def place(first, recv, start, depth, aux, rows):
    senders, _, width = recv.shape

    def slot(k):
        return pl.BlockSpec((senders, width, width), lambda p, first: (0, k * aux + start + p, 0))

    size = senders * CAP * depth * width * width
    return pl.pallas_call(
        place_kernel,
        out_shape=jax.ShapeDtypeStruct((rows, depth * width), recv.dtype),
        grid_spec=pltpu.PrefetchScalarGridSpec(
            num_scalar_prefetch=1,
            grid=(depth,),
            in_specs=[slot(k) for k in range(CAP)],
            out_specs=pl.BlockSpec((rows, width), lambda p, first: (0, p)),
            scratch_shapes=[pltpu.VMEM((rows, width), jnp.float32)],
        ),
        compiler_params=pltpu.CompilerParams(vmem_limit_bytes=8 * 1024 * 1024),
        cost_estimate=pl.CostEstimate(flops=size, bytes_accessed=4 * size, transcendentals=0),
        name="place",
    )(first, *[recv] * CAP)


FROM = (0, -1, 1, 2)


def hop(x, by, first):
    pairs = []
    for device in range(128):
        xl, y, xh, core = device // 16 % 2, device // 4 % 4, device // 2 % 2, device % 2
        if (core == 0) == first:
            to = device + ((y + by) % 4 - y) * 4
        else:
            to_x = (2 * xh + xl + by) % 4
            to = device + (to_x % 2 - xl) * 16 + (to_x // 2 - xh) * 2
        pairs.append((device, to))
    return lax.ppermute(x, AXES, pairs)


def ring(x, first):
    return [x] + [hop(x, by, first) for by in (1, -1, 2)]


def lay_kernel(spots, *refs):
    pieces, out_ref = refs[:-1], refs[-1]
    z, y, core = lax.axis_index("z"), lax.axis_index("y"), lax.axis_index("core")
    x = 2 * lax.axis_index("xh") + lax.axis_index("xl")
    for piece, (side, dz, start) in zip(pieces, spots, strict=True):
        source = (core + side) % 2
        for i in range(piece.shape[0]):
            late, early = FROM[(start + i) // 4], FROM[(start + i) % 4]
            to_x = (x + 4 + late + (early - late) * source) % 4
            to_y = (y + 4 + early + (late - early) * source) % 4
            out_ref[(z + 4 + dz) % 4, to_x % 2, to_y, to_x // 2, source] = piece[i]


def lay(spots, pieces):
    _, rows, columns = pieces[0].shape
    out = pl.pallas_call(
        functools.partial(lay_kernel, spots),
        out_shape=jax.ShapeDtypeStruct((*SIZES, rows, columns), pieces[0].dtype),
        in_specs=[pl.BlockSpec(memory_space=pltpu.VMEM)] * len(pieces),
        out_specs=pl.BlockSpec(memory_space=pltpu.VMEM),
        compiler_params=pltpu.CompilerParams(vmem_limit_bytes=20 * 1024 * 1024),
        cost_estimate=pl.CostEstimate(
            flops=0, bytes_accessed=512 * rows * columns, transcendentals=0
        ),
        name="lay",
    )(*pieces)
    return out.reshape(-1, columns)


FORWARDED = ((0, 0), (-1, 0), (1, 0), (2, 0), (2, 8))
DIRECT = ((0, 0), (-1, 0), (1, 0), (2, 0))


def z_forwarded(mine):
    half = mine.shape[0] // 2
    below, above = up(mine), down(mine)
    return [mine, below, above, up(below[:half]), down(above[half:])]


def z_direct(mine):
    return [mine, up(mine), down(mine), up(mine, 2)]


def assemble(spots, pieces, copies):
    spots = [(side, *spot) for side in range(2) for spot in spots]
    return lay(spots, pieces + copies)


def pair_kernel(x_ref, *refs):
    y_refs, out_ref = refs[:-1], refs[-1]
    blocks, width, _ = x_ref.shape
    aux_x = x_ref.shape[2] // width
    same = lax.broadcasted_iota(jnp.int32, (width, width), 0) == lax.broadcasted_iota(
        jnp.int32, (width, width), 1
    )
    x = jnp.concatenate(
        [
            jnp.concatenate(
                [x_ref[k, :, p * width : (p + 1) * width] for k in range(blocks)], axis=1
            )
            for p in range(aux_x)
        ],
        axis=0,
    )
    done = 0
    for y_ref in y_refs:
        products = lax.dot_general(
            x, y_ref[...], (((1,), (1,)), ((), ())), preferred_element_type=jnp.float32
        )
        aux_y = y_ref.shape[0] // width
        for q in range(aux_y):
            for p in range(aux_x):
                tile = products[p * width : (p + 1) * width, q * width : (q + 1) * width]
                tile = jnp.where(same, tile, 0.0).reshape(width // 8, 8, width)
                out_ref[(done + q) * aux_x + p] = tile.sum(axis=0)
        done += aux_y


def pair_sums(x, ys):
    _, width, _ = x.shape
    aux_x, aux_y = x.shape[2] // width, sum(y.shape[0] for y in ys) // width
    sums = pl.pallas_call(
        pair_kernel,
        out_shape=jax.ShapeDtypeStruct((aux_y * aux_x, 8, width), jnp.float32),
        in_specs=[pl.BlockSpec(memory_space=pltpu.VMEM)] * (1 + len(ys)),
        out_specs=pl.BlockSpec(memory_space=pltpu.VMEM),
        compiler_params=pltpu.CompilerParams(vmem_limit_bytes=16 * 1024 * 1024),
        cost_estimate=pl.CostEstimate(
            flops=2 * x.size * aux_y, bytes_accessed=6 * x.size, transcendentals=0
        ),
        name="pair",
    )(x, *ys)
    return sums.sum(axis=(1, 2)).reshape(aux_y, aux_x).T


def col_sum(x):
    x = x + other_core(x)
    x = x + permute(x, "xh", lambda k: 1 - k)
    x = x + permute(x, "y", lambda k: k ^ 1)
    return x + permute(x, "y", lambda k: 3 - k)


def shards(tensor_blocks, block_list, occ_green, virt_green):
    col_count = lax.axis_size(COL)
    blocks = tensor_blocks[0]
    aux, width = blocks.shape[1], blocks.shape[-1]
    basis_total = occ_green.shape[1]
    shard_rows = occ_green.shape[0]

    picked = pick(block_list[0], blocks, col_count)
    line = ring(jnp.concatenate([occ_green, virt_green.T], axis=0)[None], True)
    plane = ring(jnp.concatenate(line, axis=0), False)
    picked, plane = lax.optimization_barrier((picked, plane))
    plane = jnp.concatenate(plane, axis=0)
    recv = lax.all_to_all(picked, COL, split_axis=0, concat_axis=0, tiled=True)
    notes = CAP * aux * width
    recv_first = recv[:, notes : notes + CAP, 0].astype(jnp.int32).reshape(-1) - 1

    occ_plane, virt_plane = plane[:, :shard_rows], plane[:, shard_rows:]
    occ_pieces = z_forwarded(occ_plane)
    occ_pieces, virt_plane = lax.optimization_barrier((occ_pieces, virt_plane))
    virt_pieces = z_direct(virt_plane)
    occ = assemble(FORWARDED, occ_pieces, [other_core(p) for p in occ_pieces])

    dense, turned, start = [], [], 0
    for depth in CHUNKS:
        dense.append(place(recv_first, recv, start, depth, aux, basis_total))
        half = jnp.dot(occ, dense[-1], preferred_element_type=jnp.float32).astype(jnp.bfloat16)
        cut = half.reshape(col_count, width, -1)
        turned.append(lax.all_to_all(cut, COL, split_axis=0, concat_axis=0, tiled=True))
        start += depth

    _, virt_pieces = lax.optimization_barrier((half, virt_pieces))
    virt_copies = [other_core(p) for p in virt_pieces]
    turned[0], virt_copies = lax.optimization_barrier((turned[0], virt_copies))
    virt_t = assemble(DIRECT, virt_pieces, virt_copies)
    virt_half = [
        lax.dot_general(
            d, virt_t, (((0,), (0,)), ((), ())), preferred_element_type=jnp.float32
        ).astype(jnp.bfloat16)
        for d in dense
    ]
    sums = jnp.concatenate([pair_sums(x, virt_half) for x in turned], axis=0)
    return (col_sum(sums) / float(basis_total))[None]


def solution(mesh):
    fine = Mesh(mesh.devices.reshape(SIZES), AXES)
    in_specs = (
        P(ROW, COL, None, None, None),
        P(ROW, COL, None),
        P(ROW + COL, None),
        P(None, ROW + COL),
    )
    return jax.shard_map(
        shards, mesh=fine, in_specs=in_specs, out_specs=P(ROW, None, None), check_vma=False
    )
```

```python
import functools

import jax
import jax.numpy as jnp
from jax import lax
from jax.experimental import pallas as pl
from jax.experimental.pallas import tpu as pltpu
from jax.sharding import Mesh
from jax.sharding import PartitionSpec as P

CAP = 2
CHUNKS = (3, 3)
NOTE = 16
AXES = ("z", "xl", "y", "xh", "core")
SIZES = (4, 2, 4, 2, 2)
COL = ("y", "xh", "core")
ROW = ("z", "xl")


def moved(axis, to):
    where = AXES.index(axis)
    stride = 1
    for size in SIZES[where + 1 :]:
        stride *= size
    total = 1
    for size in SIZES:
        total *= size
    pairs = []
    for device in range(total):
        k = device // stride % SIZES[where]
        pairs.append((device, device + (to(k) - k) * stride))
    return pairs


def permute(x, axis, to):
    return lax.ppermute(x, AXES, moved(axis, to))


def up(x, by=1):
    return permute(x, "z", lambda k: (k + by) % 4)


def down(x):
    return permute(x, "z", lambda k: (k - 1) % 4)


def other_core(x):
    return permute(x, "core", lambda k: 1 - k)


def pick_kernel(pairs_ref, blocks_ref, out_ref, count, first):
    held, rows, width = blocks_ref.shape
    owners = count.shape[0]
    for d in range(owners):
        count[d] = 0
        for k in range(CAP):
            first[d, k] = 0

    def body(t, carry):
        l = pairs_ref[t, 1]
        k = count[l]
        count[l] = k + 1
        first[l, k] = pairs_ref[t, 0] + 1
        out_ref[l, pl.ds(pl.multiple_of(k * rows, rows), rows), :] = blocks_ref[t]
        return carry

    lax.fori_loop(0, held, body, 0)
    which = lax.broadcasted_iota(jnp.int32, (NOTE, width), 0)
    for d in range(owners):
        note = jnp.zeros((NOTE, width), jnp.float32)
        for k in range(CAP):
            note = jnp.where(which == k, first[d, k].astype(jnp.float32), note)
        out_ref[d, CAP * rows :, :] = note.astype(out_ref.dtype)


def pick(pairs, blocks, owners):
    held, aux, width, _ = blocks.shape
    rows = aux * width
    return pl.pallas_call(
        pick_kernel,
        out_shape=jax.ShapeDtypeStruct((owners, CAP * rows + NOTE, width), blocks.dtype),
        in_specs=[
            pl.BlockSpec(memory_space=pltpu.SMEM),
            pl.BlockSpec(memory_space=pltpu.VMEM),
        ],
        out_specs=pl.BlockSpec(memory_space=pltpu.VMEM),
        scratch_shapes=[
            pltpu.SMEM((owners,), jnp.int32),
            pltpu.SMEM((owners, CAP), jnp.int32),
        ],
        compiler_params=pltpu.CompilerParams(vmem_limit_bytes=16 * 1024 * 1024),
        cost_estimate=pl.CostEstimate(flops=0, bytes_accessed=4 * blocks.size, transcendentals=0),
        name="pick",
    )(pairs, blocks.reshape(held, rows, width))


def place_kernel(first_ref, *refs):
    slot_refs, out_ref, total = refs[:CAP], refs[CAP], refs[CAP + 1]
    width = total.shape[1]
    total[...] = jnp.zeros_like(total)

    def body(s, carry):
        for k, slots in enumerate(slot_refs):
            m = first_ref[s * CAP + k]

            @pl.when(m >= 0)
            def _():
                rows = pl.ds(pl.multiple_of(m * width, width), width)
                total[rows, :] += slots[s].astype(jnp.float32)

        return carry

    lax.fori_loop(0, slot_refs[0].shape[0], body, 0, unroll=True)
    out_ref[...] = total[...].astype(out_ref.dtype)


def place(first, recv, start, depth, aux, rows):
    senders, _, width = recv.shape

    def slot(k):
        return pl.BlockSpec((senders, width, width), lambda p, first: (0, k * aux + start + p, 0))

    size = senders * CAP * depth * width * width
    return pl.pallas_call(
        place_kernel,
        out_shape=jax.ShapeDtypeStruct((rows, depth * width), recv.dtype),
        grid_spec=pltpu.PrefetchScalarGridSpec(
            num_scalar_prefetch=1,
            grid=(depth,),
            in_specs=[slot(k) for k in range(CAP)],
            out_specs=pl.BlockSpec((rows, width), lambda p, first: (0, p)),
            scratch_shapes=[pltpu.VMEM((rows, width), jnp.float32)],
        ),
        compiler_params=pltpu.CompilerParams(vmem_limit_bytes=8 * 1024 * 1024),
        cost_estimate=pl.CostEstimate(flops=size, bytes_accessed=4 * size, transcendentals=0),
        name="place",
    )(first, *[recv] * CAP)


FROM = (0, -1, 1, 2)


def hop(x, by, first):
    pairs = []
    for device in range(128):
        xl, y, xh, core = device // 16 % 2, device // 4 % 4, device // 2 % 2, device % 2
        if (core == 0) == first:
            to = device + ((y + by) % 4 - y) * 4
        else:
            to_x = (2 * xh + xl + by) % 4
            to = device + (to_x % 2 - xl) * 16 + (to_x // 2 - xh) * 2
        pairs.append((device, to))
    return lax.ppermute(x, AXES, pairs)


def ring(x, first):
    return [x] + [hop(x, by, first) for by in (1, -1, 2)]


def lay_kernel(spots, *refs):
    pieces, out_ref = refs[:-1], refs[-1]
    z, y, core = lax.axis_index("z"), lax.axis_index("y"), lax.axis_index("core")
    x = 2 * lax.axis_index("xh") + lax.axis_index("xl")
    for piece, (side, dz, start) in zip(pieces, spots, strict=True):
        source = (core + side) % 2
        for i in range(piece.shape[0]):
            late, early = FROM[(start + i) // 4], FROM[(start + i) % 4]
            to_x = (x + 4 + late + (early - late) * source) % 4
            to_y = (y + 4 + early + (late - early) * source) % 4
            out_ref[(z + 4 + dz) % 4, to_x % 2, to_y, to_x // 2, source] = piece[i]


def lay(spots, pieces):
    _, rows, columns = pieces[0].shape
    out = pl.pallas_call(
        functools.partial(lay_kernel, spots),
        out_shape=jax.ShapeDtypeStruct((*SIZES, rows, columns), pieces[0].dtype),
        in_specs=[pl.BlockSpec(memory_space=pltpu.VMEM)] * len(pieces),
        out_specs=pl.BlockSpec(memory_space=pltpu.VMEM),
        compiler_params=pltpu.CompilerParams(vmem_limit_bytes=20 * 1024 * 1024),
        cost_estimate=pl.CostEstimate(
            flops=0, bytes_accessed=512 * rows * columns, transcendentals=0
        ),
        name="lay",
    )(*pieces)
    return out.reshape(-1, columns)


FORWARDED = ((0, 0), (-1, 0), (1, 0), (2, 0), (2, 8))
DIRECT = ((0, 0), (-1, 0), (1, 0), (2, 0))


def z_forwarded(mine):
    half = mine.shape[0] // 2
    below, above = up(mine), down(mine)
    return [mine, below, above, up(below[:half]), down(above[half:])]


def z_direct(mine):
    return [mine, up(mine), down(mine), up(mine, 2)]


def assemble(spots, pieces, copies):
    spots = [(side, *spot) for side in range(2) for spot in spots]
    return lay(spots, pieces + copies)


def pair_kernel(x_ref, *refs):
    y_refs, out_ref = refs[:-1], refs[-1]
    blocks, width, _ = x_ref.shape
    aux_x = x_ref.shape[2] // width
    same = lax.broadcasted_iota(jnp.int32, (width, width), 0) == lax.broadcasted_iota(
        jnp.int32, (width, width), 1
    )
    x = jnp.concatenate(
        [
            jnp.concatenate(
                [x_ref[k, :, p * width : (p + 1) * width] for k in range(blocks)], axis=1
            )
            for p in range(aux_x)
        ],
        axis=0,
    )
    done = 0
    for y_ref in y_refs:
        products = lax.dot_general(
            x, y_ref[...], (((1,), (1,)), ((), ())), preferred_element_type=jnp.float32
        )
        aux_y = y_ref.shape[0] // width
        for q in range(aux_y):
            for p in range(aux_x):
                tile = products[p * width : (p + 1) * width, q * width : (q + 1) * width]
                tile = jnp.where(same, tile, 0.0).reshape(width // 8, 8, width)
                out_ref[(done + q) * aux_x + p] = tile.sum(axis=0)
        done += aux_y


def pair_sums(x, ys):
    _, width, _ = x.shape
    aux_x, aux_y = x.shape[2] // width, sum(y.shape[0] for y in ys) // width
    sums = pl.pallas_call(
        pair_kernel,
        out_shape=jax.ShapeDtypeStruct((aux_y * aux_x, 8, width), jnp.float32),
        in_specs=[pl.BlockSpec(memory_space=pltpu.VMEM)] * (1 + len(ys)),
        out_specs=pl.BlockSpec(memory_space=pltpu.VMEM),
        compiler_params=pltpu.CompilerParams(vmem_limit_bytes=16 * 1024 * 1024),
        cost_estimate=pl.CostEstimate(
            flops=2 * x.size * aux_y, bytes_accessed=6 * x.size, transcendentals=0
        ),
        name="pair",
    )(x, *ys)
    return sums.sum(axis=(1, 2)).reshape(aux_y, aux_x).T


def col_sum(x):
    x = x + other_core(x)
    x = x + permute(x, "xh", lambda k: 1 - k)
    x = x + permute(x, "y", lambda k: k ^ 1)
    return x + permute(x, "y", lambda k: 3 - k)


def shards(tensor_blocks, block_list, occ_green, virt_green):
    col_count = lax.axis_size(COL)
    blocks = tensor_blocks[0]
    aux, width = blocks.shape[1], blocks.shape[-1]
    basis_total = occ_green.shape[1]
    shard_rows = occ_green.shape[0]

    picked = pick(block_list[0], blocks, col_count)
    line = ring(jnp.concatenate([occ_green, virt_green.T], axis=0)[None], True)
    plane = ring(jnp.concatenate(line, axis=0), False)
    picked, plane = lax.optimization_barrier((picked, plane))
    plane = jnp.concatenate(plane, axis=0)
    recv = lax.all_to_all(picked, COL, split_axis=0, concat_axis=0, tiled=True)
    notes = CAP * aux * width
    recv_first = recv[:, notes : notes + CAP, 0].astype(jnp.int32).reshape(-1) - 1

    occ_plane, virt_plane = plane[:, :shard_rows], plane[:, shard_rows:]
    occ_pieces = z_forwarded(occ_plane)
    occ_pieces, virt_plane = lax.optimization_barrier((occ_pieces, virt_plane))
    virt_pieces = z_direct(virt_plane)
    occ = assemble(FORWARDED, occ_pieces, [other_core(p) for p in occ_pieces])

    dense, turned, start = [], [], 0
    for depth in CHUNKS:
        dense.append(place(recv_first, recv, start, depth, aux, basis_total))
        half = jnp.dot(occ, dense[-1], preferred_element_type=jnp.float32).astype(jnp.bfloat16)
        cut = half.reshape(col_count, width, -1)
        turned.append(lax.all_to_all(cut, COL, split_axis=0, concat_axis=0, tiled=True))
        start += depth

    _, virt_pieces = lax.optimization_barrier((half, virt_pieces))
    virt_copies = [other_core(p) for p in virt_pieces]
    turned[0], virt_copies = lax.optimization_barrier((turned[0], virt_copies))
    virt_t = assemble(DIRECT, virt_pieces, virt_copies)
    virt_half = [
        lax.dot_general(
            d, virt_t, (((0,), (0,)), ((), ())), preferred_element_type=jnp.float32
        ).astype(jnp.bfloat16)
        for d in dense
    ]
    virt_half = [jnp.concatenate(virt_half, axis=0)]
    sums = jnp.concatenate([pair_sums(x, virt_half) for x in turned], axis=0)
    return (col_sum(sums) / float(basis_total))[None]


def solution(mesh):
    fine = Mesh(mesh.devices.reshape(SIZES), AXES)
    in_specs = (
        P(ROW, COL, None, None, None),
        P(ROW, COL, None),
        P(ROW + COL, None),
        P(None, ROW + COL),
    )
    return jax.shard_map(
        shards, mesh=fine, in_specs=in_specs, out_specs=P(ROW, None, None), check_vma=False
    )
```
